32 devices in a mesh: groups: 2 (over x), paths: 16 (over z, y, core).
Axes of the slice: x: 2, y: 2, z: 4, core: 2. Of those that a mesh axis runs over, the one named last changes fastest.
Arguments:
- path_basis: bfloat16 [4096, 512], P(('groups', 'paths')), parts along dimension 0, may hold values from -6 to 6
- proxy_weight: bfloat16 [4096, 512], P(('groups', 'paths')), parts along dimension 0, may hold values from -0.25 to 0.25
- notional: bfloat16 [4096], P(('groups', 'paths')), parts along dimension 0, may hold values from -4 to 4
- set_of: int32 [4096], P('groups'), parts along dimension 0, may hold values from 0 to 511
- threshold_index: int32 [1024], P('groups'), parts along dimension 0, may hold values from 0 to 15
- threshold_levels: float32 [32], P('groups'), parts along dimension 0, may hold values from 0.5 to 20
- loss_rate: float32 [1024], P('groups'), parts along dimension 0, may hold values from 0.4 to 1
Outputs:
- expected_loss: float32 [2], P('groups'), parts along dimension 0
- basis_adjoint: float32 [4096, 512], P(('groups', 'paths')), parts along dimension 0
- weight_adjoint: float32 [4096, 512], P(('groups', 'paths')), parts along dimension 0
The draws below stay inside these ranges and needn't reach their ends.
There are 2 independent parts, one for each index of `groups`. The reference program is written for one: setup_inputs(seed, part) draws one part's arguments, and reference() takes and returns one part's arrays. A program takes and returns all parts, laid end to end along the dimension named above; each array names one. Nothing has to cross between parts.
Inputs may be any that keep to these rules, and one draw needn't show every extreme that they name: `set_of`: netting set of each trade; set sizes are uneven.
All inputs are finite; a program needn't handle non-finite values.
Results may differ from the reference program's by a relative error of at most 0.0041.
Values may be sent and summed in bfloat16 or wider, within the bound.
A program may use at most 64 MiB of HBM per device.

```python
import math
import jax
import jax.numpy as jnp
import numpy as np
from jax import lax

FEATURES = 512
TRADES = 2048
SETS = 512
REGRESSORS = 32
LEVELS = 16
PATHS = 2048


def plant(array, rng, smallest, high):
    spot = [jax.random.randint(jax.random.fold_in(rng, axis), (), 0, length) for axis, length in enumerate(array.shape)]
    main_axis = array.shape.index(max(array.shape))
    next_to = spot[:main_axis] + [(spot[main_axis] + 1) % array.shape[main_axis]] + spot[main_axis + 1:]
    return array.at[tuple(spot)].set(smallest).at[tuple(next_to)].set(high)


def block_scale(key, extent, shards, smallest, high):
    def one(dim, parts):
        heights = jax.random.uniform(jax.random.fold_in(jax.random.fold_in(key, 6), dim), (parts,), jnp.float32, smallest / len(shards), high / len(shards))
        return jnp.repeat(jnp.exp(heights), extent[dim] // parts).reshape((-1,) + (1,) * (len(extent) - dim - 1))

    level = one(*shards[0])
    for cut in shards[1:]:
        level = level * one(*cut)
    return level


def rank_bounds(number_of, slope):
    portions = [(1 << 20) // math.isqrt(standing ** slope) + 1 for standing in range(1, number_of + 1)]
    deviation = 1 + sum(portions) // (1 << 30)
    return np.cumsum(np.array([max(1, weight // deviation) for weight in portions]))


def ranked(own_key, shape, count, lean):
    grid = rank_bounds(count, lean)
    pick = jax.random.randint(jax.random.fold_in(own_key, 1), shape, 0, int(grid[count - 1]))
    standing = jnp.searchsorted(jnp.asarray(grid, jnp.int32), pick, side="right")
    return jax.random.permutation(jax.random.fold_in(own_key, 2), count)[standing].astype(jnp.int32)


def gaussian(stream_key, dims, spread, most, cuts=(), kind=jnp.bfloat16):
    level = block_scale(stream_key, dims, cuts, -0.22, 0.18) if cuts else 1.0
    entries = jax.random.normal(stream_key, dims, jnp.float32) * spread * level
    return jnp.minimum(jnp.maximum(entries, -most), most).astype(kind)


def setup_inputs(seed: int = 0, part: int = 0) -> dict:
    key_list = jax.random.split(jax.random.key(seed), 8)
    part_keys = jax.random.split(jax.random.fold_in(key_list[7], part), 8)
    return {
        "path_basis": gaussian(part_keys[0], (PATHS, FEATURES), 1.0, 6.0, ((0, 16),)),
        "proxy_weight": gaussian(part_keys[1], (TRADES, FEATURES), FEATURES ** -0.5, 0.25, ((0, 16),)),
        "notional": jnp.clip(jax.random.uniform(part_keys[2], (TRADES,), jnp.float32, -4.0, 4.0) * block_scale(part_keys[2], (TRADES,), ((0, 16),), -0.4, 0.0), -4.0, 4.0).astype(jnp.bfloat16),
        "set_of": plant(ranked(part_keys[3], (TRADES,), SETS, 2), jax.random.fold_in(part_keys[3], 3), 0, SETS - 1).astype(jnp.int32),
        "threshold_index": plant(jax.random.randint(part_keys[4], (SETS,), 0, LEVELS), jax.random.fold_in(part_keys[4], 1), 0, LEVELS - 1).astype(jnp.int32),
        "threshold_levels": jnp.clip(jnp.exp(jax.random.uniform(part_keys[5], (LEVELS,), jnp.float32, math.log(0.5), math.log(20.0))), 0.5, 20.0),
        "loss_rate": jnp.clip(jax.random.uniform(part_keys[6], (SETS,), jnp.float32, 0.4, 1.0), 0.4, 1.0),
    }


RIDGE_SCALE = 0.01
PRECISE = lax.Precision.HIGHEST

def table_rows(labels, classes, target_type):
    return (labels[:, None] == jnp.arange(classes, dtype=jnp.int32)[None, :]).astype(target_type)

def contract_rows(former, latter):
    return lax.dot_general(former.astype(jnp.float32), latter.astype(jnp.float32), (((0,), (0,)), ((), ())), precision=PRECISE, preferred_element_type=jnp.float32)

def contract_cols(former, latter):
    return lax.dot_general(former.astype(jnp.float32), latter.astype(jnp.float32), (((1,), (1,)), ((), ())), precision=PRECISE, preferred_element_type=jnp.float32)

def matrix_product(former, latter):
    return jnp.dot(former.astype(jnp.float32), latter.astype(jnp.float32), precision=PRECISE, preferred_element_type=jnp.float32)

def spd_solve(matrix, target):
    lower_factor = jnp.linalg.cholesky(matrix)
    halfway = lax.linalg.triangular_solve(lower_factor, target, left_side=True, lower=True)
    return lax.linalg.triangular_solve(lower_factor, halfway, left_side=True, lower=True, transpose_a=True)

def reference(path_basis, proxy_weight, notional, set_of, threshold_index, threshold_levels, loss_rate):
    path_count = path_basis.shape[0]
    trade_count, feature_count = proxy_weight.shape
    set_total = loss_rate.shape[0]
    block_cols = math.gcd(256, trade_count)
    block_count = trade_count // block_cols
    weight_blocks = proxy_weight.reshape(block_count, block_cols, feature_count)
    notional_blocks = notional.astype(jnp.float32).reshape(block_count, block_cols)
    set_blocks = set_of.reshape(block_count, block_cols)

    def forward_step(running, pieces):
        weight_block, notional_block, set_block = pieces
        pre_act = lax.dot_general(path_basis.astype(jnp.float32), weight_block.astype(jnp.float32), (((1,), (1,)), ((), ())), preferred_element_type=jnp.float32)
        trade_value = (notional_block[None, :] * jax.nn.softplus(pre_act)).astype(jnp.bfloat16)
        return (running + jnp.dot(trade_value.astype(jnp.float32), table_rows(set_block, set_total, jnp.bfloat16).astype(jnp.float32), preferred_element_type=jnp.float32), None)
    exposure, _ = lax.scan(forward_step, jnp.zeros((path_count, set_total), jnp.float32), (weight_blocks, notional_blocks, set_blocks))
    thresholds = lax.optimization_barrier(jnp.sum(table_rows(threshold_index, threshold_levels.shape[0], jnp.float32) * threshold_levels[None, :], axis=1))
    design = jnp.concatenate([jnp.ones((path_count, 1), jnp.float32), path_basis[:, :REGRESSORS - 1].astype(jnp.float32)], axis=1)
    gram_matrix = contract_rows(design, design) + RIDGE_SCALE * path_count * jnp.eye(REGRESSORS, dtype=jnp.float32)
    coeffs = spd_solve(gram_matrix, contract_rows(design, exposure))
    fitted = matrix_product(design, coeffs)
    excess = fitted - thresholds[None, :]
    expected_loss = (jnp.sum(loss_rate[None, :] * jax.nn.softplus(excess)) / (path_count * set_total)).reshape(1)
    seed_adjoint = loss_rate[None, :] * jax.nn.sigmoid(excess)
    solve_adjoint = spd_solve(gram_matrix, contract_rows(design, seed_adjoint))
    adjoint_full = matrix_product(design, solve_adjoint)
    exposure_adjoint = adjoint_full.astype(jnp.bfloat16)
    design_adjoint = contract_cols(seed_adjoint - adjoint_full, coeffs) + contract_cols(exposure - fitted, solve_adjoint)

    def backward_step(running, pieces):
        weight_block, notional_block, set_block = pieces
        pre_trans = lax.dot_general(weight_block.astype(jnp.float32), path_basis.astype(jnp.float32), (((1,), (1,)), ((), ())), preferred_element_type=jnp.float32)
        spread_trans = lax.dot_general(table_rows(set_block, set_total, jnp.bfloat16).astype(jnp.float32), exposure_adjoint.astype(jnp.float32), (((1,), (1,)), ((), ())), preferred_element_type=jnp.float32)
        slope_trans = (notional_block[:, None] * jax.nn.sigmoid(pre_trans) * spread_trans).astype(jnp.bfloat16)
        running = running + lax.dot_general(slope_trans.astype(jnp.float32), weight_block.astype(jnp.float32), (((0,), (0,)), ((), ())), preferred_element_type=jnp.float32)
        return (running, jnp.dot(slope_trans.astype(jnp.float32), path_basis.astype(jnp.float32), preferred_element_type=jnp.float32))
    back_total, weight_rows = lax.scan(backward_step, jnp.zeros((path_count, feature_count), jnp.float32), (weight_blocks, notional_blocks, set_blocks))
    padding = jnp.zeros((path_count, feature_count - REGRESSORS + 1), jnp.float32)
    basis_adjoint = back_total + jnp.concatenate([design_adjoint[:, 1:], padding], axis=1)
    weight_adjoint = weight_rows.reshape(trade_count, feature_count) * (1.0 / math.sqrt(path_count))
    return (expected_loss, basis_adjoint, weight_adjoint)
```

```python
import functools
import math

import jax
import jax.numpy as jnp
from jax import lax
from jax.experimental import pallas as pl
from jax.experimental.pallas import tpu as pltpu
from jax.sharding import PartitionSpec as P

REGRESSORS = 32
RIDGE_SCALE = 0.01
PRECISE = lax.Precision.HIGHEST
LANES = 128
F32 = jnp.float32
BF16 = jnp.bfloat16

NN = (((1,), (0,)), ((), ()))
NT = (((1,), (1,)), ((), ()))
TN = (((0,), (0,)), ((), ()))


def mm(a, b, dims=NN):
    return lax.dot_general(a, b, dims, preferred_element_type=F32)


def precise(a, b, dims=NN):
    return lax.dot_general(a, b, dims, precision=PRECISE, preferred_element_type=F32)


def split3(x):
    hi = x.astype(BF16)
    rest = x - hi.astype(F32)
    mid = rest.astype(BF16)
    lo = (rest - mid.astype(F32)).astype(BF16)
    return hi, mid, lo


def stack3(x):
    hi, mid, lo = split3(x)
    return jnp.concatenate([hi, mid, lo, jnp.zeros_like(hi)], axis=0)


def design_of(basis):
    front = pltpu.roll(basis[:, :LANES].astype(F32), 1, 1)
    lane = lax.broadcasted_iota(jnp.int32, front.shape, 1)
    return jnp.where(lane == 0, 1.0, jnp.where(lane < REGRESSORS, front, 0.0))


def triple(design):
    return (
        design + pltpu.roll(design, REGRESSORS, 1) + pltpu.roll(design, 2 * REGRESSORS, 1)
    ).astype(BF16)


def spd_inverse(gram):
    size = REGRESSORS
    row = lax.broadcasted_iota(jnp.int32, (size, LANES), 0)
    lane = lax.broadcasted_iota(jnp.int32, (size, LANES), 1)
    work = jnp.where(lane < size, gram, jnp.where(lane == row + size, 1.0, 0.0))
    for k in range(size):
        column = jnp.broadcast_to(work[:, k : k + 1], work.shape)
        pivot = work[k : k + 1, :] / column[k : k + 1, :]
        work = jnp.where(row == k, pivot, work - column * pivot)
    return pltpu.roll(work, LANES - size, 1)[:, :size]


def set_table(labels, set_total):
    sets = lax.broadcasted_iota(jnp.int32, (set_total, labels.shape[1]), 0)
    return jnp.where(sets == labels, 1.0, 0.0).astype(BF16)


def kernel(
    inner, outer, paths_all, set_total,
    pb_ref, w_ref, not_ref, set_ref, tidx_ref, level_ref, rate_ref,
    loss_ref, basis_ref, wadj_ref,
    pall, wall, nall, nsend, gown, gall, gqall, gqsend,
    bown, bq, bzsend, bz, ssend, sz, agsend, ag,
    eown, eq, wown, wz, pown, pq, nsig, tval,
    zsend, zrecv, qsend, qrecv,
):
    rows, feats = pb_ref.shape
    trades = w_ref.shape[0]
    quarter = set_total // inner
    me = lax.axis_index("paths")
    q = lax.rem(me, inner)
    z = lax.div(me, inner)

    def q_peer(d):
        return lax.rem(q + d, inner)

    def z_peer(d):
        return lax.rem(z + d, outer)

    barrier = pltpu.get_barrier_semaphore()
    for d in range(1, inner):
        pl.semaphore_signal(
            barrier, inc=1, device_id={"paths": z * inner + q_peer(d)},
            device_id_type=pl.DeviceIdType.MESH,
        )
    for d in range(1, outer):
        pl.semaphore_signal(
            barrier, inc=1, device_id={"paths": z_peer(d) * inner + q},
            device_id_type=pl.DeviceIdType.MESH,
        )

    pending = []

    def over_q(which, source, target):
        copies = []
        for d in range(1, inner):
            copy = pltpu.make_async_remote_copy(
                src_ref=source(q_peer(d)), dst_ref=target.at[q],
                send_sem=qsend.at[which, d - 1], recv_sem=qrecv.at[which, d - 1],
                device_id={"paths": z * inner + q_peer(d)},
                device_id_type=pl.DeviceIdType.MESH,
            )
            copy.start()
            copies.append(copy)
        pending.extend(copies)
        return copies

    def over_z(which, source, target):
        copies = []
        for d in range(1, outer):
            copy = pltpu.make_async_remote_copy(
                src_ref=source(z_peer(d)), dst_ref=target.at[z],
                send_sem=zsend.at[which, d - 1], recv_sem=zrecv.at[which, d - 1],
                device_id={"paths": z_peer(d) * inner + q},
                device_id_type=pl.DeviceIdType.MESH,
            )
            copy.start()
            copies.append(copy)
        pending.extend(copies)
        return copies

    def arrive(copies):
        for copy in copies:
            copy.wait_recv()

    def total(ref, count):
        result = ref[0].astype(F32)
        for i in range(1, count):
            result = result + ref[i].astype(F32)
        return result

    own_design = design_of(pb_ref[...])
    own_triple = triple(own_design)
    own_bf = own_design.astype(BF16)
    nrow = jnp.broadcast_to(not_ref[...].astype(F32), (8, trades))
    nsend[...] = nrow
    gram_own = mm(own_bf, own_bf, TN)[:REGRESSORS, :]
    gown[...] = gram_own
    pl.semaphore_wait(barrier, inner + outer - 2)

    gram_z = over_z(0, lambda peer: gown, gall)
    note_z = over_z(1, lambda peer: nsend, nall)
    path_q = over_q(0, lambda peer: pb_ref, pall)
    trade_z = over_z(2, lambda peer: w_ref, wall)
    gall[z] = gram_own
    nall[z] = nrow
    pall[q] = pb_ref[...]
    wall[z] = w_ref[...]

    arrive(gram_z)
    gram_mid = total(gall, outer)
    gqsend[...] = gram_mid
    gram_q = over_q(1, lambda peer: gqsend, gqall)
    gqall[q] = gram_mid

    thresholds = jnp.zeros((1, quarter), F32)
    levels = tidx_ref[pl.ds(q, 1), :]
    all_levels = tidx_ref[...]
    all_thresholds = jnp.zeros((inner, quarter), F32)
    for i in range(level_ref.shape[0]):
        thresholds = jnp.where(levels == i, level_ref[i], thresholds)
        all_thresholds = jnp.where(all_levels == i, level_ref[i], all_thresholds)
    rate = rate_ref[pl.ds(q, 1), :]
    all_rates = rate_ref[...]
    labels = jnp.concatenate(
        [set_ref[pl.ds(i * inner + q, 1), :] for i in range(outer)], axis=1
    )
    table = set_table(labels, set_total)

    arrive(path_q)
    paths = pall[...].reshape(inner * rows, feats)
    design = design_of(paths)
    design3 = triple(design)
    design_t = jnp.transpose(design)[:REGRESSORS, :].astype(BF16)

    arrive(gram_q)
    gram_row = lax.broadcasted_iota(jnp.int32, (REGRESSORS, LANES), 0)
    gram_lane = lax.broadcasted_iota(jnp.int32, (REGRESSORS, LANES), 1)
    ridge = jnp.where(gram_row == gram_lane, RIDGE_SCALE * paths_all, 0.0)
    inverse = spd_inverse(total(gqall, inner) + ridge)

    arrive(note_z)
    notional = jnp.concatenate([nall[i][0:1, :] for i in range(outer)], axis=1)
    arrive(trade_z)
    weights = wall[...].reshape(outer * trades, feats)
    pre_act = mm(paths, weights, NT)
    small = jnp.exp(-jnp.abs(pre_act))
    tval[...] = (notional * (jnp.maximum(pre_act, 0.0) + jnp.log1p(small))).astype(BF16)
    nsig[...] = notional * (jnp.where(pre_act >= 0.0, 1.0, small) / (1.0 + small))

    by_trade = mm(design_t, tval[...])
    by_set = mm(jnp.concatenate(split3(by_trade), axis=0), table, NT)
    moments = (
        by_set[:REGRESSORS] + by_set[REGRESSORS : 2 * REGRESSORS] + by_set[2 * REGRESSORS :]
    )
    for i in range(inner):
        bown[i] = moments[:, i * quarter : (i + 1) * quarter]
    moment_q = over_q(2, lambda peer: bown.at[peer], bq)
    bq[q] = bown[q]
    arrive(moment_q)
    moment_mid = total(bq, inner)
    bzsend[...] = moment_mid
    moment_z = over_z(3, lambda peer: bzsend, bz)
    bz[z] = moment_mid
    arrive(moment_z)
    coeffs = precise(inverse, total(bz, outer))
    excess = mm(design3, stack3(coeffs)) - thresholds
    fade = jnp.exp(-jnp.abs(excess))
    loss = jnp.maximum(excess, 0.0) + jnp.log1p(fade)
    seed = rate * (jnp.where(excess >= 0.0, 1.0, fade) / (1.0 + fade))
    loss_row = rate * jnp.sum(loss, axis=0, keepdims=True)
    seed_cut = mm(design_t, jnp.concatenate(split3(seed), axis=1))
    seed_sum = (
        seed_cut[:, :quarter] + seed_cut[:, quarter : 2 * quarter] + seed_cut[:, 2 * quarter :]
    )
    message = jnp.concatenate([seed_sum, jnp.broadcast_to(loss_row, (8, quarter))], axis=0)
    ssend[...] = message
    seed_z = over_z(4, lambda peer: ssend, sz)
    sz[z] = message
    arrive(seed_z)
    seed_total = total(sz, outer)
    solved = precise(inverse, seed_total[:REGRESSORS])
    answer = jnp.concatenate([coeffs, solved, seed_total[REGRESSORS:]], axis=0)
    agsend[...] = answer
    answer_q = over_q(3, lambda peer: agsend, ag)
    ag[q] = answer
    arrive(answer_q)
    answers = jnp.concatenate([ag[i] for i in range(inner)], axis=1)
    coeffs_all = answers[:REGRESSORS]
    solved_all = answers[REGRESSORS : 2 * REGRESSORS]
    loss_sum = jnp.sum(answers[2 * REGRESSORS : 2 * REGRESSORS + 1], axis=1, keepdims=True)
    loss_ref[...] = jnp.broadcast_to(loss_sum / (paths_all * set_total), loss_ref.shape)

    picked = mm(jnp.concatenate(split3(solved_all), axis=0), table)
    solved_at = (
        picked[:REGRESSORS] + picked[REGRESSORS : 2 * REGRESSORS] + picked[2 * REGRESSORS :]
    )
    solved3 = jnp.concatenate(
        [picked.astype(BF16), jnp.zeros((LANES - 3 * REGRESSORS, picked.shape[1]), BF16)], axis=0
    )
    spread = mm(design3, solved3).astype(BF16).astype(F32)
    slopes = (nsig[...] * spread).astype(BF16)
    scale = 1.0 / math.sqrt(paths_all)
    weight_part = mm(slopes, paths, TN) * scale
    wown[...] = weight_part.astype(BF16).reshape(outer, trades, feats)
    weight_z = over_z(5, lambda peer: wown.at[peer], wz)
    wz[z] = wown[z]

    pulled = mm(solved3, tval[...], NT)
    pulled = (
        pulled[:REGRESSORS]
        + pulled[REGRESSORS : 2 * REGRESSORS]
        + pulled[2 * REGRESSORS : 3 * REGRESSORS]
    )
    for i in range(inner):
        eown[i] = pulled[:, i * rows : (i + 1) * rows]
    pull_q = over_q(4, lambda peer: eown.at[peer], eq)
    eq[q] = eown[q]
    basis_part = mm(slopes, weights)
    pown[...] = basis_part.astype(BF16).reshape(inner, rows, feats)
    basis_q = over_q(5, lambda peer: pown.at[peer], pq)
    pq[q] = pown[q]

    fitted = mm(own_triple, stack3(coeffs_all))
    full_thresholds = jnp.concatenate([all_thresholds[i : i + 1] for i in range(inner)], axis=1)
    full_rates = jnp.concatenate([all_rates[i : i + 1] for i in range(inner)], axis=1)
    over = fitted - full_thresholds
    tail = jnp.exp(-jnp.abs(over))
    own_seed = full_rates * (jnp.where(over >= 0.0, 1.0, tail) / (1.0 + tail))
    residual = own_seed - mm(own_triple, stack3(solved_all))
    term = precise(coeffs_all, residual, NT) - precise(solved_all, fitted, NT)
    arrive(pull_q)
    term = term + total(eq, inner)
    padded = jnp.concatenate([term, jnp.zeros((LANES - REGRESSORS, rows), F32)], axis=0)
    turned = pltpu.roll(jnp.transpose(padded), LANES - 1, 1)
    lane = lax.broadcasted_iota(jnp.int32, turned.shape, 1)
    turned = jnp.where(lane < REGRESSORS - 1, turned, 0.0)
    arrive(basis_q)
    basis_ref[...] = total(pq, inner)
    basis_ref[:, :LANES] = basis_ref[:, :LANES] + turned
    arrive(weight_z)
    wadj_ref[...] = total(wz, outer)
    for copy in pending:
        copy.wait_send()


def shards(
    path_basis, proxy_weight, notional, set_of, threshold_index, threshold_levels, loss_rate
):
    count = lax.axis_size("paths")
    inner = math.gcd(4, count)
    outer = count // inner
    rows, feats = path_basis.shape
    trades = proxy_weight.shape[0]
    set_total = loss_rate.shape[0]
    quarter = set_total // inner
    size = REGRESSORS
    vmem = pl.BlockSpec(memory_space=pltpu.VMEM)
    z_pairs, q_pairs = max(outer - 1, 1), max(inner - 1, 1)
    loss, basis_adjoint, weight_adjoint = pl.pallas_call(
        functools.partial(kernel, inner, outer, rows * count, set_total),
        out_shape=(
            jax.ShapeDtypeStruct((1, LANES), F32),
            jax.ShapeDtypeStruct((rows, feats), F32),
            jax.ShapeDtypeStruct((trades, feats), F32),
        ),
        in_specs=[
            vmem, vmem, vmem, vmem, vmem, pl.BlockSpec(memory_space=pltpu.SMEM), vmem,
        ],
        out_specs=(vmem, vmem, vmem),
        scratch_shapes=[
            pltpu.VMEM((inner, rows, feats), BF16),
            pltpu.VMEM((outer, trades, feats), BF16),
            pltpu.VMEM((outer, 8, trades), F32),
            pltpu.VMEM((8, trades), F32),
            pltpu.VMEM((size, LANES), F32),
            pltpu.VMEM((outer, size, LANES), F32),
            pltpu.VMEM((inner, size, LANES), F32),
            pltpu.VMEM((size, LANES), F32),
            pltpu.VMEM((inner, size, quarter), F32),
            pltpu.VMEM((inner, size, quarter), F32),
            pltpu.VMEM((size, quarter), F32),
            pltpu.VMEM((outer, size, quarter), F32),
            pltpu.VMEM((size + 8, quarter), F32),
            pltpu.VMEM((outer, size + 8, quarter), F32),
            pltpu.VMEM((2 * size + 8, quarter), F32),
            pltpu.VMEM((inner, 2 * size + 8, quarter), F32),
            pltpu.VMEM((inner, size, rows), F32),
            pltpu.VMEM((inner, size, rows), F32),
            pltpu.VMEM((outer, trades, feats), BF16),
            pltpu.VMEM((outer, trades, feats), BF16),
            pltpu.VMEM((inner, rows, feats), BF16),
            pltpu.VMEM((inner, rows, feats), BF16),
            pltpu.VMEM((inner * rows, outer * trades), F32),
            pltpu.VMEM((inner * rows, outer * trades), BF16),
            pltpu.SemaphoreType.DMA((6, z_pairs)),
            pltpu.SemaphoreType.DMA((6, z_pairs)),
            pltpu.SemaphoreType.DMA((6, q_pairs)),
            pltpu.SemaphoreType.DMA((6, q_pairs)),
        ],
        compiler_params=pltpu.CompilerParams(
            collective_id=0, has_side_effects=True, vmem_limit_bytes=48 * 1024 * 1024
        ),
    )(
        path_basis,
        proxy_weight,
        notional.reshape(1, trades),
        set_of.reshape(-1, trades),
        threshold_index.reshape(inner, quarter),
        threshold_levels,
        loss_rate.reshape(inner, quarter),
    )
    return loss[0, :1], basis_adjoint, weight_adjoint


def solution(mesh):
    placed = (
        P(("groups", "paths"), None),
        P(("groups", "paths"), None),
        P(("groups", "paths")),
        P("groups"),
        P("groups"),
        P("groups"),
        P("groups"),
    )
    return jax.shard_map(
        shards,
        mesh=mesh,
        in_specs=placed,
        out_specs=(P("groups"), P(("groups", "paths"), None), P(("groups", "paths"), None)),
        check_vma=False,
    )
```

```python
import functools
import math

import jax
import jax.numpy as jnp
from jax import lax
from jax.experimental import pallas as pl
from jax.experimental.pallas import tpu as pltpu
from jax.sharding import PartitionSpec as P

REGRESSORS = 32
RIDGE_SCALE = 0.01
PRECISE = lax.Precision.HIGHEST
LANES = 128
F32 = jnp.float32
BF16 = jnp.bfloat16

NN = (((1,), (0,)), ((), ()))
NT = (((1,), (1,)), ((), ()))
TN = (((0,), (0,)), ((), ()))


def mm(a, b, dims=NN):
    return lax.dot_general(a, b, dims, preferred_element_type=F32)


def precise(a, b, dims=NN):
    return lax.dot_general(a, b, dims, precision=PRECISE, preferred_element_type=F32)


def split3(x):
    hi = x.astype(BF16)
    rest = x - hi.astype(F32)
    mid = rest.astype(BF16)
    lo = (rest - mid.astype(F32)).astype(BF16)
    return hi, mid, lo


def stack3(x):
    hi, mid, lo = split3(x)
    return jnp.concatenate([hi, mid, lo, jnp.zeros_like(hi)], axis=0)


def design_of(basis):
    front = pltpu.roll(basis[:, :LANES].astype(F32), 1, 1)
    lane = lax.broadcasted_iota(jnp.int32, front.shape, 1)
    return jnp.where(lane == 0, 1.0, jnp.where(lane < REGRESSORS, front, 0.0))


def triple(design):
    return (
        design + pltpu.roll(design, REGRESSORS, 1) + pltpu.roll(design, 2 * REGRESSORS, 1)
    ).astype(BF16)


def spd_inverse(gram):
    size = REGRESSORS
    row = lax.broadcasted_iota(jnp.int32, (size, LANES), 0)
    lane = lax.broadcasted_iota(jnp.int32, (size, LANES), 1)
    work = jnp.where(lane < size, gram, jnp.where(lane == row + size, 1.0, 0.0))
    for k in range(size):
        column = jnp.broadcast_to(work[:, k : k + 1], work.shape)
        pivot = work[k : k + 1, :] / column[k : k + 1, :]
        work = jnp.where(row == k, pivot, work - column * pivot)
    return pltpu.roll(work, LANES - size, 1)


def set_table(labels, set_total):
    sets = lax.broadcasted_iota(jnp.int32, (set_total, labels.shape[1]), 0)
    return jnp.where(sets == labels, 1.0, 0.0).astype(BF16)


def partner(index, step, count):
    if count & (count - 1):
        return lax.rem(index + step, count)
    result, weight = 0, 1
    while weight < count:
        bit = lax.rem(lax.div(index, weight), 2)
        result = result + weight * (1 - bit if step & weight else bit)
        weight *= 2
    return result


def kernel(
    inner, outer, paths_all, set_total,
    pb_hbm, w_hbm, not_hbm, set_hbm, tidx_hbm, level_hbm, rate_hbm,
    loss_ref, basis_ref, wadj_ref,
    not_ref, set_ref, tidx_ref, level_ref, rate_ref,
    pall, wall, nall, nsend, gown, gall, gq, dstack, table, invert,
    bown, bq, bzsend, bz, csend, cq, ssend, sq,
    eown, eq, wown, wz, pown, pq, nsig, tval,
    local, zsend, zrecv, qsend, qrecv,
):
    rows, feats = basis_ref.shape
    trades = wadj_ref.shape[0]
    quarter = set_total // inner
    me = lax.axis_index("paths")
    q = lax.rem(me, inner)
    z = lax.div(me, inner)

    loads = [
        pltpu.make_async_copy(source, target, local.at[i])
        for i, (source, target) in enumerate(
            [
                (pb_hbm, pall.at[q]),
                (not_hbm, not_ref),
                (w_hbm, wall.at[z]),
                (set_hbm, set_ref),
                (tidx_hbm, tidx_ref),
                (level_hbm, level_ref),
                (rate_hbm, rate_ref),
            ]
        )
    ]
    for load in loads:
        load.start()

    barrier = pltpu.get_barrier_semaphore()
    for d in range(1, inner):
        pl.semaphore_signal(
            barrier, inc=1, device_id={"paths": z * inner + lax.rem(q + d, inner)},
            device_id_type=pl.DeviceIdType.MESH,
        )
    for d in range(1, outer):
        pl.semaphore_signal(
            barrier, inc=1, device_id={"paths": lax.rem(z + d, outer) * inner + q},
            device_id_type=pl.DeviceIdType.MESH,
        )

    pending = []

    def over_q(which, source, target):
        copies = []
        for d in range(inner - 1, 0, -1):
            peer = partner(q, d, inner)
            copy = pltpu.make_async_remote_copy(
                src_ref=source(peer), dst_ref=target.at[q],
                send_sem=qsend.at[which, d - 1], recv_sem=qrecv.at[which, d - 1],
                device_id={"paths": z * inner + peer},
                device_id_type=pl.DeviceIdType.MESH,
            )
            copy.start()
            copies.append(copy)
        pending.extend(copies)
        return copies

    def over_z(which, source, target):
        copies = []
        for d in range(outer - 1, 0, -1):
            peer = partner(z, d, outer)
            copy = pltpu.make_async_remote_copy(
                src_ref=source(peer), dst_ref=target.at[z],
                send_sem=zsend.at[which, d - 1], recv_sem=zrecv.at[which, d - 1],
                device_id={"paths": peer * inner + q},
                device_id_type=pl.DeviceIdType.MESH,
            )
            copy.start()
            copies.append(copy)
        pending.extend(copies)
        return copies

    def arrive(copies):
        for copy in copies:
            copy.wait_recv()

    def total(ref, count):
        result = ref[0].astype(F32)
        for i in range(1, count):
            result = result + ref[i].astype(F32)
        return result

    loads[0].wait()
    own_design = design_of(pall[q])
    own_triple = triple(own_design)
    own_turned = jnp.transpose(own_design)[:REGRESSORS, :].astype(BF16)
    gown[...] = own_turned
    loads[1].wait()
    nrow = jnp.broadcast_to(not_ref[...].astype(F32), (8, trades))
    nsend[...] = nrow
    loads[2].wait()
    pl.semaphore_wait(barrier, inner + outer - 2)

    gram_z = over_z(0, lambda peer: gown, gall)
    note_z = over_z(1, lambda peer: nsend, nall)
    trade_z = over_z(2, lambda peer: wall.at[z], wall)
    path_q = over_q(0, lambda peer: pall.at[q], pall)
    gall[z] = own_turned
    nall[z] = nrow

    arrive(gram_z)
    gram_q = over_q(1, lambda peer: gall, gq)
    gq[q] = gall[...]

    for load in loads[3:]:
        load.wait()
    all_levels = tidx_ref[...]
    all_thresholds = jnp.zeros((inner, quarter), F32)
    levels = tidx_ref[pl.ds(q, 1), :]
    thresholds = jnp.zeros((1, quarter), F32)
    for i in range(level_ref.shape[0]):
        thresholds = jnp.where(levels == i, level_ref[i], thresholds)
        all_thresholds = jnp.where(all_levels == i, level_ref[i], all_thresholds)
    thresholds = jnp.transpose(jnp.broadcast_to(thresholds, (quarter, quarter)))[:, :1]
    rate = jnp.transpose(
        jnp.broadcast_to(rate_ref[pl.ds(q, 1), :], (quarter, quarter))
    )[:, :1]
    all_rates = rate_ref[...]
    labels = jnp.concatenate(
        [set_ref[pl.ds(i * inner + q, 1), :] for i in range(outer)], axis=1
    )
    table[...] = set_table(labels, set_total)

    arrive(path_q)
    paths = pall[...].reshape(inner * rows, feats)
    design = design_of(paths)
    design3 = triple(design)
    design_t = jnp.transpose(design)[:REGRESSORS, :].astype(BF16)

    arrive(gram_q)
    turned_all = jnp.concatenate(
        [gq[i, j] for i in range(inner) for j in range(outer)], axis=1
    )
    dstack[...] = jnp.concatenate(
        [turned_all, turned_all, turned_all, jnp.zeros_like(turned_all)], axis=0
    )
    gram = mm(turned_all, dstack[...], NT)
    gram_row = lax.broadcasted_iota(jnp.int32, (REGRESSORS, LANES), 0)
    gram_lane = lax.broadcasted_iota(jnp.int32, (REGRESSORS, LANES), 1)
    ridge = jnp.where(gram_row == gram_lane, RIDGE_SCALE * paths_all, 0.0)
    invert[...] = spd_inverse(gram + ridge)

    arrive(note_z)
    notional = jnp.concatenate([nall[i][0:1, :] for i in range(outer)], axis=1)
    arrive(trade_z)
    weights = wall[...].reshape(outer * trades, feats)
    pre_act = mm(paths, weights, NT)
    small = jnp.exp(-jnp.abs(pre_act))
    tval[...] = (notional * (jnp.maximum(pre_act, 0.0) + jnp.log1p(small))).astype(BF16)
    nsig[...] = notional * (jnp.where(pre_act >= 0.0, 1.0, small) / (1.0 + small))

    by_trade = mm(design_t, tval[...])
    by_set = mm(jnp.concatenate(split3(by_trade), axis=0), table[...], NT)
    moments = (
        by_set[:REGRESSORS] + by_set[REGRESSORS : 2 * REGRESSORS] + by_set[2 * REGRESSORS :]
    )
    for i in range(inner):
        bown[i] = moments[:, i * quarter : (i + 1) * quarter]
    moment_q = over_q(2, lambda peer: bown.at[peer], bq)
    bq[q] = bown[q]
    arrive(moment_q)
    moment_mid = total(bq, inner)
    bzsend[...] = moment_mid
    moment_z = over_z(3, lambda peer: bzsend, bz)
    bz[z] = moment_mid
    arrive(moment_z)
    inverse = invert[:, :REGRESSORS]
    coeffs = precise(inverse, total(bz, outer))
    csend[...] = coeffs
    coeffs_q = over_q(3, lambda peer: csend, cq)
    cq[q] = coeffs
    excess = mm(stack3(coeffs), dstack[...], TN) - thresholds
    fade = jnp.exp(-jnp.abs(excess))
    loss = jnp.maximum(excess, 0.0) + jnp.log1p(fade)
    seed = rate * (jnp.where(excess >= 0.0, 1.0, fade) / (1.0 + fade))
    seed_cut = mm(dstack[:REGRESSORS, :], jnp.concatenate(split3(seed), axis=0), NT)
    seed_sum = (
        seed_cut[:, :quarter] + seed_cut[:, quarter : 2 * quarter] + seed_cut[:, 2 * quarter :]
    )
    solved = precise(inverse, seed_sum)
    loss_part = jnp.sum(rate * jnp.sum(loss, axis=1, keepdims=True), axis=0, keepdims=True)
    answer = jnp.concatenate([solved, jnp.broadcast_to(loss_part, (8, quarter))], axis=0)
    ssend[...] = answer
    answer_q = over_q(4, lambda peer: ssend, sq)
    sq[q] = answer
    arrive(coeffs_q)
    coeffs_all = jnp.concatenate([cq[i] for i in range(inner)], axis=1)
    arrive(answer_q)
    answers = jnp.concatenate([sq[i] for i in range(inner)], axis=1)
    solved_all = answers[:REGRESSORS]
    loss_sum = jnp.sum(answers[REGRESSORS : REGRESSORS + 1], axis=1, keepdims=True) / quarter
    loss_ref[...] = jnp.broadcast_to(loss_sum / (paths_all * set_total), loss_ref.shape)

    picked = mm(jnp.concatenate(split3(solved_all), axis=0), table[...])
    solved3 = jnp.concatenate(
        [picked.astype(BF16), jnp.zeros((LANES - 3 * REGRESSORS, picked.shape[1]), BF16)], axis=0
    )
    spread = mm(design3, solved3).astype(BF16).astype(F32)
    slopes = (nsig[...] * spread).astype(BF16)
    scale = 1.0 / math.sqrt(paths_all)
    weight_part = mm(slopes, paths, TN) * scale
    wown[...] = weight_part.astype(BF16).reshape(outer, trades, feats)
    weight_z = over_z(4, lambda peer: wown.at[peer], wz)
    wz[z] = wown[z]

    pulled = mm(solved3, tval[...], NT)
    pulled = (
        pulled[:REGRESSORS]
        + pulled[REGRESSORS : 2 * REGRESSORS]
        + pulled[2 * REGRESSORS : 3 * REGRESSORS]
    )
    for i in range(inner):
        eown[i] = pulled[:, i * rows : (i + 1) * rows]
    pull_q = over_q(5, lambda peer: eown.at[peer], eq)
    eq[q] = eown[q]
    basis_part = mm(slopes, weights)
    pown[...] = basis_part.astype(BF16).reshape(inner, rows, feats)
    basis_q = over_q(6, lambda peer: pown.at[peer], pq)
    pq[q] = pown[q]

    fitted = mm(own_triple, stack3(coeffs_all))
    full_thresholds = jnp.concatenate([all_thresholds[i : i + 1] for i in range(inner)], axis=1)
    full_rates = jnp.concatenate([all_rates[i : i + 1] for i in range(inner)], axis=1)
    over = fitted - full_thresholds
    tail = jnp.exp(-jnp.abs(over))
    own_seed = full_rates * (jnp.where(over >= 0.0, 1.0, tail) / (1.0 + tail))
    residual = own_seed - mm(own_triple, stack3(solved_all))
    term = precise(coeffs_all, residual, NT) - precise(solved_all, fitted, NT)
    arrive(pull_q)
    term = term + total(eq, inner)
    padded = jnp.concatenate([term, jnp.zeros((LANES - REGRESSORS, rows), F32)], axis=0)
    turned = pltpu.roll(jnp.transpose(padded), LANES - 1, 1)
    lane = lax.broadcasted_iota(jnp.int32, turned.shape, 1)
    turned = jnp.where(lane < REGRESSORS - 1, turned, 0.0)
    arrive(basis_q)
    basis_ref[...] = total(pq, inner)
    basis_ref[:, :LANES] = basis_ref[:, :LANES] + turned
    arrive(weight_z)
    wadj_ref[...] = total(wz, outer)
    for copy in pending:
        copy.wait_send()


def shards(
    path_basis, proxy_weight, notional, set_of, threshold_index, threshold_levels, loss_rate
):
    count = lax.axis_size("paths")
    inner = math.gcd(4, count)
    outer = count // inner
    rows, feats = path_basis.shape
    trades = proxy_weight.shape[0]
    set_total = loss_rate.shape[0]
    quarter = set_total // inner
    size = REGRESSORS
    vmem = pl.BlockSpec(memory_space=pltpu.VMEM)
    z_pairs, q_pairs = max(outer - 1, 1), max(inner - 1, 1)
    loss, basis_adjoint, weight_adjoint = pl.pallas_call(
        functools.partial(kernel, inner, outer, rows * count, set_total),
        out_shape=(
            jax.ShapeDtypeStruct((1, LANES), F32),
            jax.ShapeDtypeStruct((rows, feats), F32),
            jax.ShapeDtypeStruct((trades, feats), F32),
        ),
        in_specs=[pl.BlockSpec(memory_space=pltpu.HBM)] * 7,
        out_specs=(vmem, vmem, vmem),
        scratch_shapes=[
            pltpu.VMEM((1, trades), BF16),
            pltpu.VMEM((inner * outer, trades), jnp.int32),
            pltpu.VMEM((inner, quarter), jnp.int32),
            pltpu.SMEM(threshold_levels.shape, F32),
            pltpu.VMEM((inner, quarter), F32),
            pltpu.VMEM((inner, rows, feats), BF16),
            pltpu.VMEM((outer, trades, feats), BF16),
            pltpu.VMEM((outer, 8, trades), F32),
            pltpu.VMEM((8, trades), F32),
            pltpu.VMEM((size, rows), BF16),
            pltpu.VMEM((outer, size, rows), BF16),
            pltpu.VMEM((inner, outer, size, rows), BF16),
            pltpu.VMEM((LANES, count * rows), BF16),
            pltpu.VMEM((set_total, outer * trades), BF16),
            pltpu.VMEM((size, LANES), F32),
            pltpu.VMEM((inner, size, quarter), F32),
            pltpu.VMEM((inner, size, quarter), F32),
            pltpu.VMEM((size, quarter), F32),
            pltpu.VMEM((outer, size, quarter), F32),
            pltpu.VMEM((size, quarter), F32),
            pltpu.VMEM((inner, size, quarter), F32),
            pltpu.VMEM((size + 8, quarter), F32),
            pltpu.VMEM((inner, size + 8, quarter), F32),
            pltpu.VMEM((inner, size, rows), F32),
            pltpu.VMEM((inner, size, rows), F32),
            pltpu.VMEM((outer, trades, feats), BF16),
            pltpu.VMEM((outer, trades, feats), BF16),
            pltpu.VMEM((inner, rows, feats), BF16),
            pltpu.VMEM((inner, rows, feats), BF16),
            pltpu.VMEM((inner * rows, outer * trades), F32),
            pltpu.VMEM((inner * rows, outer * trades), BF16),
            pltpu.SemaphoreType.DMA((7,)),
            pltpu.SemaphoreType.DMA((5, z_pairs)),
            pltpu.SemaphoreType.DMA((5, z_pairs)),
            pltpu.SemaphoreType.DMA((7, q_pairs)),
            pltpu.SemaphoreType.DMA((7, q_pairs)),
        ],
        compiler_params=pltpu.CompilerParams(
            collective_id=0, has_side_effects=True, vmem_limit_bytes=67043328
        ),
    )(
        path_basis,
        proxy_weight,
        notional.reshape(1, trades),
        set_of.reshape(-1, trades),
        threshold_index.reshape(inner, quarter),
        threshold_levels,
        loss_rate.reshape(inner, quarter),
    )
    return loss[0, :1], basis_adjoint, weight_adjoint


def solution(mesh):
    placed = (
        P(("groups", "paths"), None),
        P(("groups", "paths"), None),
        P(("groups", "paths")),
        P("groups"),
        P("groups"),
        P("groups"),
        P("groups"),
    )
    return jax.shard_map(
        shards,
        mesh=mesh,
        in_specs=placed,
        out_specs=(P("groups"), P(("groups", "paths"), None), P(("groups", "paths"), None)),
        check_vma=False,
    )
```

```python
import functools
import math

import jax
import jax.numpy as jnp
from jax import lax
from jax.experimental import pallas as pl
from jax.experimental.pallas import tpu as pltpu
from jax.sharding import PartitionSpec as P

REGRESSORS = 32
RIDGE_SCALE = 0.01
PRECISE = lax.Precision.HIGHEST
LANES = 128
F32 = jnp.float32
BF16 = jnp.bfloat16

NN = (((1,), (0,)), ((), ()))
NT = (((1,), (1,)), ((), ()))
TN = (((0,), (0,)), ((), ()))


def mm(a, b, dims=NN):
    return lax.dot_general(a, b, dims, preferred_element_type=F32)


def precise(a, b, dims=NN):
    return lax.dot_general(a, b, dims, precision=PRECISE, preferred_element_type=F32)


def split3(x):
    hi = x.astype(BF16)
    rest = x - hi.astype(F32)
    mid = rest.astype(BF16)
    lo = (rest - mid.astype(F32)).astype(BF16)
    return hi, mid, lo


def stack3(x):
    hi, mid, lo = split3(x)
    return jnp.concatenate([hi, mid, lo, jnp.zeros_like(hi)], axis=0)


def design_of(basis):
    front = pltpu.roll(basis[:, :LANES].astype(F32), 1, 1)
    lane = lax.broadcasted_iota(jnp.int32, front.shape, 1)
    return jnp.where(lane == 0, 1.0, jnp.where(lane < REGRESSORS, front, 0.0))


def triple(design):
    return (
        design + pltpu.roll(design, REGRESSORS, 1) + pltpu.roll(design, 2 * REGRESSORS, 1)
    ).astype(BF16)


def spd_inverse(gram):
    size = REGRESSORS
    row = lax.broadcasted_iota(jnp.int32, (size, LANES), 0)
    lane = lax.broadcasted_iota(jnp.int32, (size, LANES), 1)
    work = jnp.where(lane < size, gram, jnp.where(lane == row + size, 1.0, 0.0))
    for k in range(size):
        column = jnp.broadcast_to(work[:, k : k + 1], work.shape)
        pivot = work[k : k + 1, :] / column[k : k + 1, :]
        work = jnp.where(row == k, pivot, work - column * pivot)
    return pltpu.roll(work, LANES - size, 1)


def set_table(labels, set_total):
    sets = lax.broadcasted_iota(jnp.int32, (set_total, labels.shape[1]), 0)
    return jnp.where(sets == labels, 1.0, 0.0).astype(BF16)


def partner(index, step, count):
    if count & (count - 1):
        return lax.rem(index + step, count)
    result, weight = 0, 1
    while weight < count:
        bit = lax.rem(lax.div(index, weight), 2)
        result = result + weight * (1 - bit if step & weight else bit)
        weight *= 2
    return result


def kernel(
    inner, outer, paths_all, set_total,
    pb_hbm, w_hbm, not_hbm, set_hbm, tidx_hbm, level_hbm, rate_hbm,
    loss_ref, basis_ref, wadj_ref,
    not_ref, set_ref, tidx_ref, level_ref, rate_ref,
    pall, wall, nall, nsend, gown, gall, gq, dstack, table, invert,
    bown, bq, bzsend, bz, csend, cq, ssend, sq,
    eown, eq, wown, wz, pown, pq, nsig, tval,
    local, zsend, zrecv, qsend, qrecv,
):
    rows, feats = basis_ref.shape
    trades = wadj_ref.shape[0]
    quarter = set_total // inner
    me = lax.axis_index("paths")
    q = lax.rem(me, inner)
    z = lax.div(me, inner)

    loads = [
        pltpu.make_async_copy(source, target, local.at[i])
        for i, (source, target) in enumerate(
            [
                (pb_hbm, pall.at[q]),
                (not_hbm, not_ref),
                (w_hbm, wall.at[z]),
                (set_hbm, set_ref),
                (tidx_hbm, tidx_ref),
                (level_hbm, level_ref),
                (rate_hbm, rate_ref),
            ]
        )
    ]
    for load in loads:
        load.start()

    barrier = pltpu.get_barrier_semaphore()
    for d in range(1, inner):
        pl.semaphore_signal(
            barrier, inc=1, device_id={"paths": z * inner + lax.rem(q + d, inner)},
            device_id_type=pl.DeviceIdType.MESH,
        )
    for d in range(1, outer):
        pl.semaphore_signal(
            barrier, inc=1, device_id={"paths": lax.rem(z + d, outer) * inner + q},
            device_id_type=pl.DeviceIdType.MESH,
        )

    pending = []

    def over_q(which, source, target):
        copies = []
        for d in range(inner - 1, 0, -1):
            peer = partner(q, d, inner)
            copy = pltpu.make_async_remote_copy(
                src_ref=source(peer), dst_ref=target.at[q],
                send_sem=qsend.at[which, d - 1], recv_sem=qrecv.at[which, d - 1],
                device_id={"paths": z * inner + peer},
                device_id_type=pl.DeviceIdType.MESH,
            )
            copy.start()
            copies.append(copy)
        pending.extend(copies)
        return copies

    def over_z(which, source, target):
        copies = []
        for d in range(outer - 1, 0, -1):
            peer = partner(z, d, outer)
            copy = pltpu.make_async_remote_copy(
                src_ref=source(peer), dst_ref=target.at[z],
                send_sem=zsend.at[which, d - 1], recv_sem=zrecv.at[which, d - 1],
                device_id={"paths": peer * inner + q},
                device_id_type=pl.DeviceIdType.MESH,
            )
            copy.start()
            copies.append(copy)
        pending.extend(copies)
        return copies

    def arrive(copies):
        for copy in copies:
            copy.wait_recv()

    def total(ref, count):
        result = ref[0].astype(F32)
        for i in range(1, count):
            result = result + ref[i].astype(F32)
        return result

    loads[0].wait()
    own_design = design_of(pall[q])
    own_triple = triple(own_design)
    own_turned = jnp.transpose(own_design)[:REGRESSORS, :].astype(BF16)
    gown[...] = own_turned
    loads[1].wait()
    nrow = jnp.broadcast_to(not_ref[...].astype(F32), (8, trades))
    nsend[...] = nrow
    loads[2].wait()
    pl.semaphore_wait(barrier, inner + outer - 2)

    gram_z = over_z(0, lambda peer: gown, gall)
    note_z = over_z(1, lambda peer: nsend, nall)
    trade_z = over_z(2, lambda peer: wall.at[z], wall)
    path_q = over_q(0, lambda peer: pall.at[q], pall)
    gall[z] = own_turned
    nall[z] = nrow

    arrive(gram_z)
    gram_q = over_q(1, lambda peer: gall, gq)
    gq[q] = gall[...]

    for load in loads[3:]:
        load.wait()
    all_levels = tidx_ref[...]
    all_thresholds = jnp.zeros((inner, quarter), F32)
    levels = tidx_ref[pl.ds(q, 1), :]
    thresholds = jnp.zeros((1, quarter), F32)
    for i in range(level_ref.shape[0]):
        thresholds = jnp.where(levels == i, level_ref[i], thresholds)
        all_thresholds = jnp.where(all_levels == i, level_ref[i], all_thresholds)
    thresholds = jnp.transpose(jnp.broadcast_to(thresholds, (quarter, quarter)))[:, :1]
    rate = jnp.transpose(
        jnp.broadcast_to(rate_ref[pl.ds(q, 1), :], (quarter, quarter))
    )[:, :1]
    all_rates = rate_ref[...]
    labels = jnp.concatenate(
        [set_ref[pl.ds(i * inner + q, 1), :] for i in range(outer)], axis=1
    )
    table[...] = set_table(labels, set_total)

    arrive(path_q)
    paths = pall[...].reshape(inner * rows, feats)
    design = design_of(paths)
    design3 = triple(design)
    design_t = jnp.transpose(design)[:REGRESSORS, :].astype(BF16)

    arrive(gram_q)
    turned_all = jnp.concatenate(
        [gq[i, j] for i in range(inner) for j in range(outer)], axis=1
    )
    dstack[...] = jnp.concatenate(
        [turned_all, turned_all, turned_all, jnp.zeros_like(turned_all)], axis=0
    )
    gram = mm(turned_all, dstack[...], NT)
    gram_row = lax.broadcasted_iota(jnp.int32, (REGRESSORS, LANES), 0)
    gram_lane = lax.broadcasted_iota(jnp.int32, (REGRESSORS, LANES), 1)
    ridge = jnp.where(gram_row == gram_lane, RIDGE_SCALE * paths_all, 0.0)
    invert[...] = spd_inverse(gram + ridge)

    arrive(note_z)
    notional = jnp.concatenate([nall[i][0:1, :] for i in range(outer)], axis=1)
    arrive(trade_z)
    weights = wall[...].reshape(outer * trades, feats)
    pre_act = mm(paths, weights, NT)
    small = jnp.exp(-jnp.abs(pre_act))
    tval[...] = (notional * (jnp.maximum(pre_act, 0.0) + jnp.log1p(small))).astype(BF16)
    nsig[...] = notional * (jnp.where(pre_act >= 0.0, 1.0, small) / (1.0 + small))

    by_trade = mm(design_t, tval[...])
    by_set = mm(jnp.concatenate(split3(by_trade), axis=0), table[...], NT)
    moments = (
        by_set[:REGRESSORS] + by_set[REGRESSORS : 2 * REGRESSORS] + by_set[2 * REGRESSORS :]
    )
    for i in range(inner):
        bown[i] = moments[:, i * quarter : (i + 1) * quarter]
    moment_q = over_q(2, lambda peer: bown.at[peer], bq)
    bq[q] = bown[q]
    arrive(moment_q)
    moment_mid = total(bq, inner)
    bzsend[...] = moment_mid
    moment_z = over_z(3, lambda peer: bzsend, bz)
    bz[z] = moment_mid
    arrive(moment_z)
    inverse = invert[:, :REGRESSORS]
    coeffs = precise(inverse, total(bz, outer))
    csend[...] = coeffs
    coeffs_q = over_q(3, lambda peer: csend, cq)
    cq[q] = coeffs
    excess = mm(stack3(coeffs), dstack[...], TN) - thresholds
    fade = jnp.exp(-jnp.abs(excess))
    loss = jnp.maximum(excess, 0.0) + jnp.log1p(fade)
    seed = rate * (jnp.where(excess >= 0.0, 1.0, fade) / (1.0 + fade))
    seed_cut = mm(dstack[:REGRESSORS, :], jnp.concatenate(split3(seed), axis=0), NT)
    seed_sum = (
        seed_cut[:, :quarter] + seed_cut[:, quarter : 2 * quarter] + seed_cut[:, 2 * quarter :]
    )
    solved = precise(inverse, seed_sum)
    loss_part = jnp.sum(rate * jnp.sum(loss, axis=1, keepdims=True), axis=0, keepdims=True)
    answer = jnp.concatenate([solved, jnp.broadcast_to(loss_part, (8, quarter))], axis=0)
    ssend[...] = answer
    answer_q = over_q(4, lambda peer: ssend, sq)
    sq[q] = answer
    arrive(coeffs_q)
    coeffs_all = jnp.concatenate([cq[i] for i in range(inner)], axis=1)
    arrive(answer_q)
    answers = jnp.concatenate([sq[i] for i in range(inner)], axis=1)
    solved_all = answers[:REGRESSORS]
    loss_sum = jnp.sum(answers[REGRESSORS : REGRESSORS + 1], axis=1, keepdims=True) / quarter
    loss_ref[...] = jnp.broadcast_to(loss_sum / (paths_all * set_total), loss_ref.shape)

    picked = mm(jnp.concatenate(split3(solved_all), axis=0), table[...])
    solved3 = jnp.concatenate(
        [picked.astype(BF16), jnp.zeros((LANES - 3 * REGRESSORS, picked.shape[1]), BF16)], axis=0
    )
    spread = mm(design3, solved3).astype(BF16).astype(F32)
    slopes = (nsig[...] * spread).astype(BF16)
    scale = 1.0 / math.sqrt(paths_all)
    weight_part = mm(slopes, paths, TN) * scale
    wown[...] = weight_part.astype(BF16).reshape(outer, trades, feats)
    weight_z = over_z(4, lambda peer: wown.at[peer], wz)
    wz[z] = wown[z]

    pulled = mm(solved3, tval[...], NT)
    pulled = (
        pulled[:REGRESSORS]
        + pulled[REGRESSORS : 2 * REGRESSORS]
        + pulled[2 * REGRESSORS : 3 * REGRESSORS]
    )
    for i in range(inner):
        eown[i] = pulled[:, i * rows : (i + 1) * rows]
    pull_q = over_q(5, lambda peer: eown.at[peer], eq)
    eq[q] = eown[q]
    basis_part = mm(slopes, weights)
    pown[...] = basis_part.astype(BF16).reshape(inner, rows, feats)
    basis_q = over_q(6, lambda peer: pown.at[peer], pq)
    pq[q] = pown[q]

    fitted = mm(own_triple, stack3(coeffs_all))
    full_thresholds = jnp.concatenate([all_thresholds[i : i + 1] for i in range(inner)], axis=1)
    full_rates = jnp.concatenate([all_rates[i : i + 1] for i in range(inner)], axis=1)
    over = fitted - full_thresholds
    tail = jnp.exp(-jnp.abs(over))
    own_seed = full_rates * (jnp.where(over >= 0.0, 1.0, tail) / (1.0 + tail))
    residual = own_seed - mm(own_triple, stack3(solved_all))
    term = precise(coeffs_all, residual, NT) - precise(solved_all, fitted, NT)
    arrive(pull_q)
    term = term + total(eq, inner)
    padded = jnp.concatenate([term, jnp.zeros((LANES - REGRESSORS, rows), F32)], axis=0)
    turned = pltpu.roll(jnp.transpose(padded), LANES - 1, 1)
    lane = lax.broadcasted_iota(jnp.int32, turned.shape, 1)
    turned = jnp.where(lane < REGRESSORS - 1, turned, 0.0)
    arrive(basis_q)
    basis_ref[...] = total(pq, inner)
    basis_ref[:, :LANES] = basis_ref[:, :LANES] + turned
    arrive(weight_z)
    wadj_ref[...] = total(wz, outer)
    for copy in pending:
        copy.wait_send()


def shards(
    path_basis, proxy_weight, notional, set_of, threshold_index, threshold_levels, loss_rate
):
    count = lax.axis_size("paths")
    inner = math.gcd(4, count)
    outer = count // inner
    rows, feats = path_basis.shape
    trades = proxy_weight.shape[0]
    set_total = loss_rate.shape[0]
    quarter = set_total // inner
    size = REGRESSORS
    vmem = pl.BlockSpec(memory_space=pltpu.VMEM)
    z_pairs, q_pairs = max(outer - 1, 1), max(inner - 1, 1)
    loss, basis_adjoint, weight_adjoint = pl.pallas_call(
        functools.partial(kernel, inner, outer, rows * count, set_total),
        out_shape=(
            jax.ShapeDtypeStruct((1, LANES), F32),
            jax.ShapeDtypeStruct((rows, feats), F32),
            jax.ShapeDtypeStruct((trades, feats), F32),
        ),
        in_specs=[pl.BlockSpec(memory_space=pltpu.HBM)] * 7,
        out_specs=(vmem, vmem, vmem),
        scratch_shapes=[
            pltpu.VMEM((1, trades), BF16),
            pltpu.VMEM((inner * outer, trades), jnp.int32),
            pltpu.VMEM((inner, quarter), jnp.int32),
            pltpu.SMEM(threshold_levels.shape, F32),
            pltpu.VMEM((inner, quarter), F32),
            pltpu.VMEM((inner, rows, feats), BF16),
            pltpu.VMEM((outer, trades, feats), BF16),
            pltpu.VMEM((outer, 8, trades), F32),
            pltpu.VMEM((8, trades), F32),
            pltpu.VMEM((size, rows), BF16),
            pltpu.VMEM((outer, size, rows), BF16),
            pltpu.VMEM((inner, outer, size, rows), BF16),
            pltpu.VMEM((LANES, count * rows), BF16),
            pltpu.VMEM((set_total, outer * trades), BF16),
            pltpu.VMEM((size, LANES), F32),
            pltpu.VMEM((inner, size, quarter), F32),
            pltpu.VMEM((inner, size, quarter), F32),
            pltpu.VMEM((size, quarter), F32),
            pltpu.VMEM((outer, size, quarter), F32),
            pltpu.VMEM((size, quarter), F32),
            pltpu.VMEM((inner, size, quarter), F32),
            pltpu.VMEM((size + 8, quarter), F32),
            pltpu.VMEM((inner, size + 8, quarter), F32),
            pltpu.VMEM((inner, size, rows), F32),
            pltpu.VMEM((inner, size, rows), F32),
            pltpu.VMEM((outer, trades, feats), BF16),
            pltpu.VMEM((outer, trades, feats), BF16),
            pltpu.VMEM((inner, rows, feats), BF16),
            pltpu.VMEM((inner, rows, feats), BF16),
            pltpu.VMEM((inner * rows, outer * trades), F32),
            pltpu.VMEM((inner * rows, outer * trades), BF16),
            pltpu.SemaphoreType.DMA((7,)),
            pltpu.SemaphoreType.DMA((5, z_pairs)),
            pltpu.SemaphoreType.DMA((5, z_pairs)),
            pltpu.SemaphoreType.DMA((7, q_pairs)),
            pltpu.SemaphoreType.DMA((7, q_pairs)),
        ],
        compiler_params=pltpu.CompilerParams(
            collective_id=0, has_side_effects=True, vmem_limit_bytes=48 * 1024 * 1024
        ),
    )(
        *(
            pltpu.with_memory_space_constraint(operand, pltpu.HBM)
            for operand in (
                path_basis,
                proxy_weight,
                notional.reshape(1, trades),
                set_of.reshape(-1, trades),
                threshold_index.reshape(inner, quarter),
                threshold_levels,
                loss_rate.reshape(inner, quarter),
            )
        )
    )
    return loss[0, :1], basis_adjoint, weight_adjoint


def solution(mesh):
    placed = (
        P(("groups", "paths"), None),
        P(("groups", "paths"), None),
        P(("groups", "paths")),
        P("groups"),
        P("groups"),
        P("groups"),
        P("groups"),
    )
    return jax.shard_map(
        shards,
        mesh=mesh,
        in_specs=placed,
        out_specs=(P("groups"), P(("groups", "paths"), None), P(("groups", "paths"), None)),
        check_vma=False,
    )
```

```python
import functools
import math

import jax
import jax.numpy as jnp
from jax import lax
from jax.experimental import pallas as pl
from jax.experimental.pallas import tpu as pltpu
from jax.sharding import PartitionSpec as P

REGRESSORS = 32
RIDGE_SCALE = 0.01
PRECISE = lax.Precision.HIGHEST
LANES = 128
PIECES = 4
F32 = jnp.float32
BF16 = jnp.bfloat16

NN = (((1,), (0,)), ((), ()))
NT = (((1,), (1,)), ((), ()))
TN = (((0,), (0,)), ((), ()))


def mm(a, b, dims=NN):
    return lax.dot_general(a, b, dims, preferred_element_type=F32)


def precise(a, b, dims=NN):
    return lax.dot_general(a, b, dims, precision=PRECISE, preferred_element_type=F32)


def split3(x):
    hi = x.astype(BF16)
    rest = x - hi.astype(F32)
    mid = rest.astype(BF16)
    lo = (rest - mid.astype(F32)).astype(BF16)
    return hi, mid, lo


def stack3(x):
    hi, mid, lo = split3(x)
    return jnp.concatenate([hi, mid, lo, jnp.zeros_like(hi)], axis=0)


def design_of(basis):
    front = pltpu.roll(basis[:, :LANES].astype(F32), 1, 1)
    lane = lax.broadcasted_iota(jnp.int32, front.shape, 1)
    return jnp.where(lane == 0, 1.0, jnp.where(lane < REGRESSORS, front, 0.0))


def triple(design):
    return (
        design + pltpu.roll(design, REGRESSORS, 1) + pltpu.roll(design, 2 * REGRESSORS, 1)
    ).astype(BF16)


def spd_inverse(gram, between):
    size = REGRESSORS
    row = lax.broadcasted_iota(jnp.int32, (size, LANES), 0)
    lane = lax.broadcasted_iota(jnp.int32, (size, LANES), 1)
    work = jnp.where(lane < size, gram, jnp.where(lane == row + size, 1.0, 0.0))
    for k in range(size):
        if k == size // 3:
            between()
        column = jnp.broadcast_to(work[:, k : k + 1], work.shape)
        pivot = work[k : k + 1, :] / column[k : k + 1, :]
        work = jnp.where(row == k, pivot, work - column * pivot)
    return pltpu.roll(work, LANES - size, 1)


def set_table(labels, set_total):
    sets = lax.broadcasted_iota(jnp.int32, (set_total, labels.shape[1]), 0)
    return jnp.where(sets == labels, 1.0, 0.0).astype(BF16)


def partner(index, step, count):
    if count & (count - 1):
        return lax.rem(index + step, count)
    result, weight = 0, 1
    while weight < count:
        bit = lax.rem(lax.div(index, weight), 2)
        result = result + weight * (1 - bit if step & weight else bit)
        weight *= 2
    return result


def kernel(
    inner, outer, paths_all, set_total,
    pb_hbm, w_hbm, not_hbm, set_hbm, tidx_hbm, level_hbm, rate_hbm,
    loss_ref, basis_ref, wadj_ref,
    not_ref, set_ref, tidx_ref, level_ref, rate_ref,
    pall, wall, nall, nsend, gown, gall, gq, dstack, table, invert,
    bown, bq, bzsend, bz, csend, cq, ssend, sq,
    eown, eq, wown, wz, pown, pq, nsig, tval,
    via, local, zsend, zrecv, qsend, qrecv, steps,
):
    rows, feats = basis_ref.shape
    trades = wadj_ref.shape[0]
    quarter = set_total // inner
    me = lax.axis_index("paths")
    q = lax.rem(me, inner)
    z = lax.div(me, inner)

    loads = [
        pltpu.make_async_copy(source, target, local.at[i])
        for i, (source, target) in enumerate(
            [
                (pb_hbm, pall.at[q]),
                (not_hbm, not_ref),
                (w_hbm, wall.at[z]),
                (set_hbm, set_ref),
                (tidx_hbm, tidx_ref),
                (level_hbm, level_ref),
                (rate_hbm, rate_ref),
            ]
        )
    ]
    for load in loads:
        load.start()

    barrier = pltpu.get_barrier_semaphore()
    for d in range(1, inner):
        pl.semaphore_signal(
            barrier, inc=1, device_id={"paths": z * inner + lax.rem(q + d, inner)},
            device_id_type=pl.DeviceIdType.MESH,
        )
    for d in range(1, outer):
        pl.semaphore_signal(
            barrier, inc=1, device_id={"paths": lax.rem(z + d, outer) * inner + q},
            device_id_type=pl.DeviceIdType.MESH,
        )

    pending = []

    def over_q(which, source, target):
        copies = []
        for d in range(inner - 1, 0, -1):
            peer = partner(q, d, inner)
            copy = pltpu.make_async_remote_copy(
                src_ref=source(peer), dst_ref=target.at[q],
                send_sem=qsend.at[which, d - 1], recv_sem=qrecv.at[which, d - 1],
                device_id={"paths": z * inner + peer},
                device_id_type=pl.DeviceIdType.MESH,
            )
            copy.start()
            copies.append(copy)
        pending.extend(copies)
        return copies

    def over_z(which, source, target):
        copies = []
        for d in range(outer - 1, 0, -1):
            peer = partner(z, d, outer)
            copy = pltpu.make_async_remote_copy(
                src_ref=source(peer), dst_ref=target.at[z],
                send_sem=zsend.at[which, d - 1], recv_sem=zrecv.at[which, d - 1],
                device_id={"paths": peer * inner + q},
                device_id_type=pl.DeviceIdType.MESH,
            )
            copy.start()
            copies.append(copy)
        pending.extend(copies)
        return copies

    def arrive(copies):
        for copy in copies:
            copy.wait_recv()

    relay = outer == 4 and trades % (16 * PIECES) == 0
    part = trades // PIECES
    edge = z * (3 - z) == 0
    near, far, mid = partner(z, 1, outer), partner(z, 2, outer), partner(z, 3, outer)

    def piece(source, target, p, row, peer):
        cut = pl.ds(p * part, part)
        return pltpu.make_async_remote_copy(
            src_ref=source.at[cut], dst_ref=target.at[cut],
            send_sem=steps.at[row, p], recv_sem=steps.at[row + 1, p],
            device_id={"paths": peer * inner + q}, device_id_type=pl.DeviceIdType.MESH,
        )

    def block(source, target, which, lane, peer):
        return pltpu.make_async_remote_copy(
            src_ref=source, dst_ref=target,
            send_sem=zsend.at[which, lane], recv_sem=zrecv.at[which, lane],
            device_id={"paths": peer * inner + q}, device_id_type=pl.DeviceIdType.MESH,
        )

    def total(ref, count):
        result = ref[0].astype(F32)
        for i in range(1, count):
            result = result + ref[i].astype(F32)
        return result

    loads[0].wait()
    own_design = design_of(pall[q])
    own_triple = triple(own_design)
    own_turned = jnp.transpose(own_design)[:REGRESSORS, :].astype(BF16)
    gown[...] = own_turned
    loads[1].wait()
    nrow = jnp.broadcast_to(not_ref[...].astype(F32), (8, trades))
    nsend[...] = nrow
    loads[2].wait()
    pl.semaphore_wait(barrier, inner + outer - 2)

    gram_z = over_z(0, lambda peer: gown, gall)
    note_z = over_z(1, lambda peer: nsend, nall)
    if relay:
        far_in = [piece(wall.at[z], wall.at[z], p, 0, far) for p in range(PIECES)]
        near_in = block(wall.at[z], wall.at[z], 2, 0, near)
        mid_in = block(wall.at[z], wall.at[z], 2, 1, mid)
        handed = [piece(wall.at[far], wall.at[far], p, 2, near) for p in range(PIECES)]
        for copy in far_in:
            copy.start()
        near_in.start()
        pending.extend(far_in + [near_in])

        @pl.when(jnp.logical_not(edge))
        def _():
            mid_in.start()
    else:
        trade_z = over_z(2, lambda peer: wall.at[z], wall)

    def forward(p):
        if relay:
            far_in[p].wait_recv()

            @pl.when(jnp.logical_not(edge))
            def _():
                handed[p].start()

    path_q = over_q(0, lambda peer: pall.at[q], pall)
    gall[z] = own_turned
    nall[z] = nrow

    arrive(gram_z)
    gram_q = over_q(1, lambda peer: gall, gq)
    gq[q] = gall[...]

    for load in loads[3:]:
        load.wait()
    all_levels = tidx_ref[...]
    all_thresholds = jnp.zeros((inner, quarter), F32)
    levels = tidx_ref[pl.ds(q, 1), :]
    thresholds = jnp.zeros((1, quarter), F32)
    for i in range(level_ref.shape[0]):
        thresholds = jnp.where(levels == i, level_ref[i], thresholds)
        all_thresholds = jnp.where(all_levels == i, level_ref[i], all_thresholds)
    thresholds = jnp.transpose(jnp.broadcast_to(thresholds, (quarter, quarter)))[:, :1]
    rate = jnp.transpose(
        jnp.broadcast_to(rate_ref[pl.ds(q, 1), :], (quarter, quarter))
    )[:, :1]
    all_rates = rate_ref[...]
    labels = jnp.concatenate(
        [set_ref[pl.ds(i * inner + q, 1), :] for i in range(outer)], axis=1
    )
    table[...] = set_table(labels, set_total)

    forward(0)
    arrive(path_q)
    paths = pall[...].reshape(inner * rows, feats)
    design = design_of(paths)
    design3 = triple(design)
    design_t = jnp.transpose(design)[:REGRESSORS, :].astype(BF16)

    forward(1)
    arrive(gram_q)
    turned_all = jnp.concatenate(
        [gq[i, j] for i in range(inner) for j in range(outer)], axis=1
    )
    dstack[...] = jnp.concatenate(
        [turned_all, turned_all, turned_all, jnp.zeros_like(turned_all)], axis=0
    )
    gram = mm(turned_all, dstack[...], NT)
    forward(2)
    gram_row = lax.broadcasted_iota(jnp.int32, (REGRESSORS, LANES), 0)
    gram_lane = lax.broadcasted_iota(jnp.int32, (REGRESSORS, LANES), 1)
    ridge = jnp.where(gram_row == gram_lane, RIDGE_SCALE * paths_all, 0.0)
    invert[...] = spd_inverse(gram + ridge, lambda: forward(3))

    arrive(note_z)
    notional = jnp.concatenate([nall[i][0:1, :] for i in range(outer)], axis=1)
    if relay:
        near_in.wait_recv()

        @pl.when(jnp.logical_not(edge))
        def _():
            mid_in.wait_recv()

        @pl.when(edge)
        def _():
            for copy in handed:
                copy.wait_recv()
    else:
        arrive(trade_z)
    weights = wall[...].reshape(outer * trades, feats)
    pre_act = mm(paths, weights, NT)
    small = jnp.exp(-jnp.abs(pre_act))
    tval[...] = (notional * (jnp.maximum(pre_act, 0.0) + jnp.log1p(small))).astype(BF16)
    nsig[...] = notional * (jnp.where(pre_act >= 0.0, 1.0, small) / (1.0 + small))

    by_trade = mm(design_t, tval[...])
    by_set = mm(jnp.concatenate(split3(by_trade), axis=0), table[...], NT)
    moments = (
        by_set[:REGRESSORS] + by_set[REGRESSORS : 2 * REGRESSORS] + by_set[2 * REGRESSORS :]
    )
    for i in range(inner):
        bown[i] = moments[:, i * quarter : (i + 1) * quarter]
    moment_q = over_q(2, lambda peer: bown.at[peer], bq)
    bq[q] = bown[q]
    arrive(moment_q)
    moment_mid = total(bq, inner)
    bzsend[...] = moment_mid
    moment_z = over_z(3, lambda peer: bzsend, bz)
    bz[z] = moment_mid
    arrive(moment_z)
    inverse = invert[:, :REGRESSORS]
    coeffs = precise(inverse, total(bz, outer))
    csend[...] = coeffs
    coeffs_q = over_q(3, lambda peer: csend, cq)
    cq[q] = coeffs
    excess = mm(stack3(coeffs), dstack[...], TN) - thresholds
    fade = jnp.exp(-jnp.abs(excess))
    loss = jnp.maximum(excess, 0.0) + jnp.log1p(fade)
    seed = rate * (jnp.where(excess >= 0.0, 1.0, fade) / (1.0 + fade))
    seed_cut = mm(dstack[:REGRESSORS, :], jnp.concatenate(split3(seed), axis=0), NT)
    seed_sum = (
        seed_cut[:, :quarter] + seed_cut[:, quarter : 2 * quarter] + seed_cut[:, 2 * quarter :]
    )
    solved = precise(inverse, seed_sum)
    loss_part = jnp.sum(rate * jnp.sum(loss, axis=1, keepdims=True), axis=0, keepdims=True)
    answer = jnp.concatenate([solved, jnp.broadcast_to(loss_part, (8, quarter))], axis=0)
    ssend[...] = answer
    answer_q = over_q(4, lambda peer: ssend, sq)
    sq[q] = answer
    arrive(coeffs_q)
    coeffs_all = jnp.concatenate([cq[i] for i in range(inner)], axis=1)
    arrive(answer_q)
    answers = jnp.concatenate([sq[i] for i in range(inner)], axis=1)
    solved_all = answers[:REGRESSORS]
    loss_sum = jnp.sum(answers[REGRESSORS : REGRESSORS + 1], axis=1, keepdims=True) / quarter
    loss_ref[...] = jnp.broadcast_to(loss_sum / (paths_all * set_total), loss_ref.shape)

    picked = mm(jnp.concatenate(split3(solved_all), axis=0), table[...])
    solved3 = jnp.concatenate(
        [picked.astype(BF16), jnp.zeros((LANES - 3 * REGRESSORS, picked.shape[1]), BF16)], axis=0
    )
    spread = mm(design3, solved3).astype(BF16).astype(F32)
    slopes = (nsig[...] * spread).astype(BF16)
    scale = 1.0 / math.sqrt(paths_all)
    weight_part = mm(slopes, paths, TN) * scale
    wown[...] = weight_part.astype(BF16).reshape(outer, trades, feats)
    if relay:
        carried = [piece(wown.at[mid], via, p, 6, near) for p in range(PIECES)]
        far_out = [piece(wown.at[far], wz.at[z], p, 4, far) for p in range(PIECES)]
        near_out = block(wown.at[near], wz.at[z], 4, 0, near)
        mid_out = block(wown.at[mid], wz.at[z], 4, 1, mid)

        @pl.when(edge)
        def _():
            for copy in carried:
                copy.start()
            for copy in far_out:
                copy.start()
            wz[mid] = jnp.zeros_like(via)

        @pl.when(jnp.logical_not(edge))
        def _():
            mid_out.start()

        near_out.start()
        pending.extend(far_out + [near_out])
    else:
        weight_z = over_z(4, lambda peer: wown.at[peer], wz)
    wz[z] = wown[z]

    pulled = mm(solved3, tval[...], NT)
    pulled = (
        pulled[:REGRESSORS]
        + pulled[REGRESSORS : 2 * REGRESSORS]
        + pulled[2 * REGRESSORS : 3 * REGRESSORS]
    )
    for i in range(inner):
        eown[i] = pulled[:, i * rows : (i + 1) * rows]
    pull_q = over_q(5, lambda peer: eown.at[peer], eq)
    eq[q] = eown[q]
    basis_part = mm(slopes, weights)
    pown[...] = basis_part.astype(BF16).reshape(inner, rows, feats)
    basis_q = over_q(6, lambda peer: pown.at[peer], pq)
    pq[q] = pown[q]

    if relay:

        @pl.when(jnp.logical_not(edge))
        def _():
            for p in range(PIECES):
                carried[p].wait_recv()
                cut = pl.ds(p * part, part)
                joint = wown[far, cut, :].astype(F32) + via[cut, :].astype(F32)
                wown[far, cut, :] = joint.astype(BF16)
                far_out[p].start()

    fitted = mm(own_triple, stack3(coeffs_all))
    full_thresholds = jnp.concatenate([all_thresholds[i : i + 1] for i in range(inner)], axis=1)
    full_rates = jnp.concatenate([all_rates[i : i + 1] for i in range(inner)], axis=1)
    over = fitted - full_thresholds
    tail = jnp.exp(-jnp.abs(over))
    own_seed = full_rates * (jnp.where(over >= 0.0, 1.0, tail) / (1.0 + tail))
    residual = own_seed - mm(own_triple, stack3(solved_all))
    term = precise(coeffs_all, residual, NT) - precise(solved_all, fitted, NT)
    arrive(pull_q)
    term = term + total(eq, inner)
    padded = jnp.concatenate([term, jnp.zeros((LANES - REGRESSORS, rows), F32)], axis=0)
    turned = pltpu.roll(jnp.transpose(padded), LANES - 1, 1)
    lane = lax.broadcasted_iota(jnp.int32, turned.shape, 1)
    turned = jnp.where(lane < REGRESSORS - 1, turned, 0.0)
    arrive(basis_q)
    basis_ref[...] = total(pq, inner)
    basis_ref[:, :LANES] = basis_ref[:, :LANES] + turned
    if relay:
        arrive(far_out)
        near_out.wait_recv()

        @pl.when(jnp.logical_not(edge))
        def _():
            mid_out.wait_recv()
            mid_out.wait_send()
            mid_in.wait_send()
            for copy in handed:
                copy.wait_send()

        @pl.when(edge)
        def _():
            for copy in carried:
                copy.wait_send()
    else:
        arrive(weight_z)
    wadj_ref[...] = total(wz, outer)
    for copy in pending:
        copy.wait_send()


def shards(
    path_basis, proxy_weight, notional, set_of, threshold_index, threshold_levels, loss_rate
):
    count = lax.axis_size("paths")
    inner = math.gcd(4, count)
    outer = count // inner
    rows, feats = path_basis.shape
    trades = proxy_weight.shape[0]
    set_total = loss_rate.shape[0]
    quarter = set_total // inner
    size = REGRESSORS
    vmem = pl.BlockSpec(memory_space=pltpu.VMEM)
    z_pairs, q_pairs = max(outer - 1, 1), max(inner - 1, 1)
    loss, basis_adjoint, weight_adjoint = pl.pallas_call(
        functools.partial(kernel, inner, outer, rows * count, set_total),
        out_shape=(
            jax.ShapeDtypeStruct((1, LANES), F32),
            jax.ShapeDtypeStruct((rows, feats), F32),
            jax.ShapeDtypeStruct((trades, feats), F32),
        ),
        in_specs=[pl.BlockSpec(memory_space=pltpu.HBM)] * 7,
        out_specs=(vmem, vmem, vmem),
        scratch_shapes=[
            pltpu.VMEM((1, trades), BF16),
            pltpu.VMEM((inner * outer, trades), jnp.int32),
            pltpu.VMEM((inner, quarter), jnp.int32),
            pltpu.SMEM(threshold_levels.shape, F32),
            pltpu.VMEM((inner, quarter), F32),
            pltpu.VMEM((inner, rows, feats), BF16),
            pltpu.VMEM((outer, trades, feats), BF16),
            pltpu.VMEM((outer, 8, trades), F32),
            pltpu.VMEM((8, trades), F32),
            pltpu.VMEM((size, rows), BF16),
            pltpu.VMEM((outer, size, rows), BF16),
            pltpu.VMEM((inner, outer, size, rows), BF16),
            pltpu.VMEM((LANES, count * rows), BF16),
            pltpu.VMEM((set_total, outer * trades), BF16),
            pltpu.VMEM((size, LANES), F32),
            pltpu.VMEM((inner, size, quarter), F32),
            pltpu.VMEM((inner, size, quarter), F32),
            pltpu.VMEM((size, quarter), F32),
            pltpu.VMEM((outer, size, quarter), F32),
            pltpu.VMEM((size, quarter), F32),
            pltpu.VMEM((inner, size, quarter), F32),
            pltpu.VMEM((size + 8, quarter), F32),
            pltpu.VMEM((inner, size + 8, quarter), F32),
            pltpu.VMEM((inner, size, rows), F32),
            pltpu.VMEM((inner, size, rows), F32),
            pltpu.VMEM((outer, trades, feats), BF16),
            pltpu.VMEM((outer, trades, feats), BF16),
            pltpu.VMEM((inner, rows, feats), BF16),
            pltpu.VMEM((inner, rows, feats), BF16),
            pltpu.VMEM((inner * rows, outer * trades), F32),
            pltpu.VMEM((inner * rows, outer * trades), BF16),
            pltpu.VMEM((trades, feats), BF16),
            pltpu.SemaphoreType.DMA((7,)),
            pltpu.SemaphoreType.DMA((5, z_pairs)),
            pltpu.SemaphoreType.DMA((5, z_pairs)),
            pltpu.SemaphoreType.DMA((7, q_pairs)),
            pltpu.SemaphoreType.DMA((7, q_pairs)),
            pltpu.SemaphoreType.DMA((8, PIECES)),
        ],
        compiler_params=pltpu.CompilerParams(
            collective_id=0, has_side_effects=True, vmem_limit_bytes=48 * 1024 * 1024
        ),
    )(
        *(
            pltpu.with_memory_space_constraint(operand, pltpu.HBM)
            for operand in (
                path_basis,
                proxy_weight,
                notional.reshape(1, trades),
                set_of.reshape(-1, trades),
                threshold_index.reshape(inner, quarter),
                threshold_levels,
                loss_rate.reshape(inner, quarter),
            )
        )
    )
    return loss[0, :1], basis_adjoint, weight_adjoint


def solution(mesh):
    placed = (
        P(("groups", "paths"), None),
        P(("groups", "paths"), None),
        P(("groups", "paths")),
        P("groups"),
        P("groups"),
        P("groups"),
        P("groups"),
    )
    return jax.shard_map(
        shards,
        mesh=mesh,
        in_specs=placed,
        out_specs=(P("groups"), P(("groups", "paths"), None), P(("groups", "paths"), None)),
        check_vma=False,
    )
```

```python
import functools
import math

import jax
import jax.numpy as jnp
from jax import lax
from jax.experimental import pallas as pl
from jax.experimental.pallas import tpu as pltpu
from jax.sharding import PartitionSpec as P

REGRESSORS = 32
RIDGE_SCALE = 0.01
PRECISE = lax.Precision.HIGHEST
LANES = 128
PIECES = 4
F32 = jnp.float32
BF16 = jnp.bfloat16

NN = (((1,), (0,)), ((), ()))
NT = (((1,), (1,)), ((), ()))
TN = (((0,), (0,)), ((), ()))


def mm(a, b, dims=NN):
    return lax.dot_general(a, b, dims, preferred_element_type=F32)


def precise(a, b, dims=NN):
    return lax.dot_general(a, b, dims, precision=PRECISE, preferred_element_type=F32)


def split3(x):
    hi = x.astype(BF16)
    rest = x - hi.astype(F32)
    mid = rest.astype(BF16)
    lo = (rest - mid.astype(F32)).astype(BF16)
    return hi, mid, lo


def stack3(x):
    hi, mid, lo = split3(x)
    return jnp.concatenate([hi, mid, lo, jnp.zeros_like(hi)], axis=0)


def design_of(basis):
    front = pltpu.roll(basis[:, :LANES].astype(F32), 1, 1)
    lane = lax.broadcasted_iota(jnp.int32, front.shape, 1)
    return jnp.where(lane == 0, 1.0, jnp.where(lane < REGRESSORS, front, 0.0))


def triple(design):
    return (
        design + pltpu.roll(design, REGRESSORS, 1) + pltpu.roll(design, 2 * REGRESSORS, 1)
    ).astype(BF16)


def spd_inverse(gram, between):
    size = REGRESSORS
    row = lax.broadcasted_iota(jnp.int32, (size, LANES), 0)
    lane = lax.broadcasted_iota(jnp.int32, (size, LANES), 1)
    work = jnp.where(lane < size, gram, jnp.where(lane == row + size, 1.0, 0.0))
    for k in range(size):
        if k == size // 3:
            between()
        column = jnp.broadcast_to(work[:, k : k + 1], work.shape)
        pivot = work[k : k + 1, :] / column[k : k + 1, :]
        work = jnp.where(row == k, pivot, work - column * pivot)
    return pltpu.roll(work, LANES - size, 1)


def set_table(labels, set_total):
    sets = lax.broadcasted_iota(jnp.int32, (set_total, labels.shape[1]), 0)
    return jnp.where(sets == labels, 1.0, 0.0).astype(BF16)


def partner(index, step, count):
    if count & (count - 1):
        return lax.rem(index + step, count)
    result, weight = 0, 1
    while weight < count:
        bit = lax.rem(lax.div(index, weight), 2)
        result = result + weight * (1 - bit if step & weight else bit)
        weight *= 2
    return result


def kernel(
    inner, outer, paths_all, set_total,
    pb_hbm, w_hbm, not_hbm, set_hbm, tidx_hbm, level_hbm, rate_hbm,
    loss_ref, basis_ref, wadj_ref,
    not_ref, set_ref, tidx_ref, level_ref, rate_ref,
    pall, wall, nall, nsend, gown, gall, gq, dstack, table, invert,
    bown, bq, bzsend, bz, csend, cq, ssend, sq, lsend, lq,
    eown, eq, wown, wz, pown, pq, nsig, tval,
    via, local, zsend, zrecv, qsend, qrecv, steps,
):
    rows, feats = basis_ref.shape
    trades = wadj_ref.shape[0]
    quarter = set_total // inner
    me = lax.axis_index("paths")
    q = lax.rem(me, inner)
    z = lax.div(me, inner)

    loads = [
        pltpu.make_async_copy(source, target, local.at[i])
        for i, (source, target) in enumerate(
            [
                (pb_hbm, pall.at[q]),
                (not_hbm, not_ref),
                (w_hbm, wall.at[z]),
                (set_hbm, set_ref),
                (tidx_hbm, tidx_ref),
                (level_hbm, level_ref),
                (rate_hbm, rate_ref),
            ]
        )
    ]
    for load in loads:
        load.start()

    barrier = pltpu.get_barrier_semaphore()
    for d in range(1, inner):
        pl.semaphore_signal(
            barrier, inc=1, device_id={"paths": z * inner + lax.rem(q + d, inner)},
            device_id_type=pl.DeviceIdType.MESH,
        )
    for d in range(1, outer):
        pl.semaphore_signal(
            barrier, inc=1, device_id={"paths": lax.rem(z + d, outer) * inner + q},
            device_id_type=pl.DeviceIdType.MESH,
        )

    pending = []

    def over_q(which, source, target):
        copies = []
        for d in range(inner - 1, 0, -1):
            peer = partner(q, d, inner)
            copy = pltpu.make_async_remote_copy(
                src_ref=source(peer), dst_ref=target.at[q],
                send_sem=qsend.at[which, d - 1], recv_sem=qrecv.at[which, d - 1],
                device_id={"paths": z * inner + peer},
                device_id_type=pl.DeviceIdType.MESH,
            )
            copy.start()
            copies.append(copy)
        pending.extend(copies)
        return copies

    def over_z(which, source, target):
        copies = []
        for d in range(outer - 1, 0, -1):
            peer = partner(z, d, outer)
            copy = pltpu.make_async_remote_copy(
                src_ref=source(peer), dst_ref=target.at[z],
                send_sem=zsend.at[which, d - 1], recv_sem=zrecv.at[which, d - 1],
                device_id={"paths": peer * inner + q},
                device_id_type=pl.DeviceIdType.MESH,
            )
            copy.start()
            copies.append(copy)
        pending.extend(copies)
        return copies

    def arrive(copies):
        for copy in copies:
            copy.wait_recv()

    relay = outer == 4 and trades % (16 * PIECES) == 0
    part = trades // PIECES
    edge = z * (3 - z) == 0
    near, far, mid = partner(z, 1, outer), partner(z, 2, outer), partner(z, 3, outer)

    def piece(source, target, p, row, peer):
        cut = pl.ds(p * part, part)
        return pltpu.make_async_remote_copy(
            src_ref=source.at[cut], dst_ref=target.at[cut],
            send_sem=steps.at[row, p], recv_sem=steps.at[row + 1, p],
            device_id={"paths": peer * inner + q}, device_id_type=pl.DeviceIdType.MESH,
        )

    def block(source, target, which, lane, peer):
        return pltpu.make_async_remote_copy(
            src_ref=source, dst_ref=target,
            send_sem=zsend.at[which, lane], recv_sem=zrecv.at[which, lane],
            device_id={"paths": peer * inner + q}, device_id_type=pl.DeviceIdType.MESH,
        )

    def total(ref, count):
        result = ref[0].astype(F32)
        for i in range(1, count):
            result = result + ref[i].astype(F32)
        return result

    loads[0].wait()
    own_design = design_of(pall[q])
    own_triple = triple(own_design)
    own_turned = jnp.transpose(own_design)[:REGRESSORS, :].astype(BF16)
    gown[...] = own_turned
    loads[1].wait()
    nrow = jnp.broadcast_to(not_ref[...].astype(F32), (8, trades))
    nsend[...] = nrow
    loads[2].wait()
    pl.semaphore_wait(barrier, inner + outer - 2)

    gram_z = over_z(0, lambda peer: gown, gall)
    note_z = over_z(1, lambda peer: nsend, nall)
    if relay:
        far_in = [piece(wall.at[z], wall.at[z], p, 0, far) for p in range(PIECES)]
        near_in = block(wall.at[z], wall.at[z], 2, 0, near)
        mid_in = block(wall.at[z], wall.at[z], 2, 1, mid)
        handed = [piece(wall.at[far], wall.at[far], p, 2, near) for p in range(PIECES)]
        for copy in far_in:
            copy.start()
        near_in.start()
        pending.extend(far_in + [near_in])

        @pl.when(jnp.logical_not(edge))
        def _():
            mid_in.start()
    else:
        trade_z = over_z(2, lambda peer: wall.at[z], wall)

    def forward(p):
        if relay:
            far_in[p].wait_recv()

            @pl.when(jnp.logical_not(edge))
            def _():
                handed[p].start()

    path_q = over_q(0, lambda peer: pall.at[q], pall)
    gall[z] = own_turned
    nall[z] = nrow

    arrive(gram_z)
    gram_q = over_q(1, lambda peer: gall, gq)
    gq[q] = gall[...]

    for load in loads[3:]:
        load.wait()
    all_levels = tidx_ref[...]
    all_thresholds = jnp.zeros((inner, quarter), F32)
    levels = tidx_ref[pl.ds(q, 1), :]
    thresholds = jnp.zeros((1, quarter), F32)
    for i in range(level_ref.shape[0]):
        thresholds = jnp.where(levels == i, level_ref[i], thresholds)
        all_thresholds = jnp.where(all_levels == i, level_ref[i], all_thresholds)
    thresholds = jnp.transpose(jnp.broadcast_to(thresholds, (quarter, quarter)))[:, :1]
    rate = jnp.transpose(
        jnp.broadcast_to(rate_ref[pl.ds(q, 1), :], (quarter, quarter))
    )[:, :1]
    all_rates = rate_ref[...]
    labels = jnp.concatenate(
        [set_ref[pl.ds(i * inner + q, 1), :] for i in range(outer)], axis=1
    )
    table[...] = set_table(labels, set_total)

    forward(0)
    arrive(path_q)
    paths = pall[...].reshape(inner * rows, feats)
    design = design_of(paths)
    design3 = triple(design)
    design_t = jnp.transpose(design)[:REGRESSORS, :].astype(BF16)

    forward(1)
    arrive(gram_q)
    turned_all = jnp.concatenate(
        [gq[i, j] for i in range(inner) for j in range(outer)], axis=1
    )
    dstack[...] = jnp.concatenate(
        [turned_all, turned_all, turned_all, jnp.zeros_like(turned_all)], axis=0
    )
    gram = mm(turned_all, dstack[...], NT)
    forward(2)
    gram_row = lax.broadcasted_iota(jnp.int32, (REGRESSORS, LANES), 0)
    gram_lane = lax.broadcasted_iota(jnp.int32, (REGRESSORS, LANES), 1)
    ridge = jnp.where(gram_row == gram_lane, RIDGE_SCALE * paths_all, 0.0)
    invert[...] = spd_inverse(gram + ridge, lambda: forward(3))

    arrive(note_z)
    notional = jnp.concatenate([nall[i][0:1, :] for i in range(outer)], axis=1)
    if relay:
        near_in.wait_recv()

        @pl.when(jnp.logical_not(edge))
        def _():
            mid_in.wait_recv()

        @pl.when(edge)
        def _():
            for copy in handed:
                copy.wait_recv()
    else:
        arrive(trade_z)
    weights = wall[...].reshape(outer * trades, feats)
    pre_act = mm(paths, weights, NT)
    small = jnp.exp(-jnp.abs(pre_act))
    tval[...] = (notional * (jnp.maximum(pre_act, 0.0) + jnp.log1p(small))).astype(BF16)

    by_trade = mm(design_t, tval[...])
    by_set = mm(jnp.concatenate(split3(by_trade), axis=0), table[...], NT)
    moments = (
        by_set[:REGRESSORS] + by_set[REGRESSORS : 2 * REGRESSORS] + by_set[2 * REGRESSORS :]
    )
    for i in range(inner):
        bown[i] = moments[:, i * quarter : (i + 1) * quarter]
    moment_q = over_q(2, lambda peer: bown.at[peer], bq)
    bq[q] = bown[q]
    nsig[...] = notional * (jnp.where(pre_act >= 0.0, 1.0, small) / (1.0 + small))
    arrive(moment_q)
    moment_mid = total(bq, inner)
    bzsend[...] = moment_mid
    moment_z = over_z(3, lambda peer: bzsend, bz)
    bz[z] = moment_mid
    arrive(moment_z)
    inverse = invert[:, :REGRESSORS]
    coeffs = precise(inverse, total(bz, outer))
    csend[...] = coeffs
    coeffs_q = over_q(3, lambda peer: csend, cq)
    cq[q] = coeffs
    excess = mm(stack3(coeffs), dstack[...], TN) - thresholds
    fade = jnp.exp(-jnp.abs(excess))
    seed = rate * (jnp.where(excess >= 0.0, 1.0, fade) / (1.0 + fade))
    seed_cut = mm(dstack[:REGRESSORS, :], jnp.concatenate(split3(seed), axis=0), NT)
    seed_sum = (
        seed_cut[:, :quarter] + seed_cut[:, quarter : 2 * quarter] + seed_cut[:, 2 * quarter :]
    )
    solved = precise(inverse, seed_sum)
    ssend[...] = solved
    answer_q = over_q(4, lambda peer: ssend, sq)
    sq[q] = solved
    loss = jnp.maximum(excess, 0.0) + jnp.log1p(fade)
    loss_part = jnp.sum(rate * jnp.sum(loss, axis=1, keepdims=True), axis=0, keepdims=True)
    loss_row = jnp.broadcast_to(loss_part, (8, LANES))
    lsend[...] = loss_row
    loss_q = over_q(7, lambda peer: lsend, lq)
    lq[q] = loss_row
    arrive(coeffs_q)
    coeffs_all = jnp.concatenate([cq[i] for i in range(inner)], axis=1)
    arrive(answer_q)
    solved_all = jnp.concatenate([sq[i] for i in range(inner)], axis=1)

    picked = mm(jnp.concatenate(split3(solved_all), axis=0), table[...])
    solved3 = jnp.concatenate(
        [picked.astype(BF16), jnp.zeros((LANES - 3 * REGRESSORS, picked.shape[1]), BF16)], axis=0
    )
    spread = mm(design3, solved3).astype(BF16).astype(F32)
    slopes = (nsig[...] * spread).astype(BF16)
    scale = 1.0 / math.sqrt(paths_all)
    weight_part = mm(slopes, paths, TN) * scale
    wown[...] = weight_part.astype(BF16).reshape(outer, trades, feats)
    if relay:
        carried = [piece(wown.at[mid], via, p, 6, near) for p in range(PIECES)]
        far_out = [piece(wown.at[far], wz.at[z], p, 4, far) for p in range(PIECES)]
        near_out = block(wown.at[near], wz.at[z], 4, 0, near)
        mid_out = block(wown.at[mid], wz.at[z], 4, 1, mid)

        @pl.when(edge)
        def _():
            for copy in carried:
                copy.start()
            for copy in far_out:
                copy.start()
            wz[mid] = jnp.zeros_like(via)

        @pl.when(jnp.logical_not(edge))
        def _():
            mid_out.start()

        near_out.start()
        pending.extend(far_out + [near_out])
    else:
        weight_z = over_z(4, lambda peer: wown.at[peer], wz)
    wz[z] = wown[z]

    pulled = mm(solved3, tval[...], NT)
    pulled = (
        pulled[:REGRESSORS]
        + pulled[REGRESSORS : 2 * REGRESSORS]
        + pulled[2 * REGRESSORS : 3 * REGRESSORS]
    )
    for i in range(inner):
        eown[i] = pulled[:, i * rows : (i + 1) * rows]
    pull_q = over_q(5, lambda peer: eown.at[peer], eq)
    eq[q] = eown[q]
    basis_part = mm(slopes, weights)
    pown[...] = basis_part.astype(BF16).reshape(inner, rows, feats)
    basis_q = over_q(6, lambda peer: pown.at[peer], pq)
    pq[q] = pown[q]

    if relay:

        @pl.when(jnp.logical_not(edge))
        def _():
            for p in range(PIECES):
                carried[p].wait_recv()
                cut = pl.ds(p * part, part)
                joint = wown[far, cut, :].astype(F32) + via[cut, :].astype(F32)
                wown[far, cut, :] = joint.astype(BF16)
                far_out[p].start()

    fitted = mm(own_triple, stack3(coeffs_all))
    full_thresholds = jnp.concatenate([all_thresholds[i : i + 1] for i in range(inner)], axis=1)
    full_rates = jnp.concatenate([all_rates[i : i + 1] for i in range(inner)], axis=1)
    over = fitted - full_thresholds
    tail = jnp.exp(-jnp.abs(over))
    own_seed = full_rates * (jnp.where(over >= 0.0, 1.0, tail) / (1.0 + tail))
    residual = own_seed - mm(own_triple, stack3(solved_all))
    term = precise(coeffs_all, residual, NT) - precise(solved_all, fitted, NT)
    arrive(loss_q)
    loss_ref[...] = total(lq, inner)[:1] / (paths_all * set_total)
    arrive(pull_q)
    term = term + total(eq, inner)
    padded = jnp.concatenate([term, jnp.zeros((LANES - REGRESSORS, rows), F32)], axis=0)
    turned = pltpu.roll(jnp.transpose(padded), LANES - 1, 1)
    lane = lax.broadcasted_iota(jnp.int32, turned.shape, 1)
    turned = jnp.where(lane < REGRESSORS - 1, turned, 0.0)
    arrive(basis_q)
    basis_ref[...] = total(pq, inner)
    basis_ref[:, :LANES] = basis_ref[:, :LANES] + turned
    if relay:
        arrive(far_out)
        near_out.wait_recv()

        @pl.when(jnp.logical_not(edge))
        def _():
            mid_out.wait_recv()
            mid_out.wait_send()
            mid_in.wait_send()
            for copy in handed:
                copy.wait_send()

        @pl.when(edge)
        def _():
            for copy in carried:
                copy.wait_send()
    else:
        arrive(weight_z)
    wadj_ref[...] = total(wz, outer)
    for copy in pending:
        copy.wait_send()


def shards(
    path_basis, proxy_weight, notional, set_of, threshold_index, threshold_levels, loss_rate
):
    count = lax.axis_size("paths")
    inner = math.gcd(4, count)
    outer = count // inner
    rows, feats = path_basis.shape
    trades = proxy_weight.shape[0]
    set_total = loss_rate.shape[0]
    quarter = set_total // inner
    size = REGRESSORS
    vmem = pl.BlockSpec(memory_space=pltpu.VMEM)
    z_pairs, q_pairs = max(outer - 1, 1), max(inner - 1, 1)
    loss, basis_adjoint, weight_adjoint = pl.pallas_call(
        functools.partial(kernel, inner, outer, rows * count, set_total),
        out_shape=(
            jax.ShapeDtypeStruct((1, LANES), F32),
            jax.ShapeDtypeStruct((rows, feats), F32),
            jax.ShapeDtypeStruct((trades, feats), F32),
        ),
        in_specs=[pl.BlockSpec(memory_space=pltpu.HBM)] * 7,
        out_specs=(vmem, vmem, vmem),
        scratch_shapes=[
            pltpu.VMEM((1, trades), BF16),
            pltpu.VMEM((inner * outer, trades), jnp.int32),
            pltpu.VMEM((inner, quarter), jnp.int32),
            pltpu.SMEM(threshold_levels.shape, F32),
            pltpu.VMEM((inner, quarter), F32),
            pltpu.VMEM((inner, rows, feats), BF16),
            pltpu.VMEM((outer, trades, feats), BF16),
            pltpu.VMEM((outer, 8, trades), F32),
            pltpu.VMEM((8, trades), F32),
            pltpu.VMEM((size, rows), BF16),
            pltpu.VMEM((outer, size, rows), BF16),
            pltpu.VMEM((inner, outer, size, rows), BF16),
            pltpu.VMEM((LANES, count * rows), BF16),
            pltpu.VMEM((set_total, outer * trades), BF16),
            pltpu.VMEM((size, LANES), F32),
            pltpu.VMEM((inner, size, quarter), F32),
            pltpu.VMEM((inner, size, quarter), F32),
            pltpu.VMEM((size, quarter), F32),
            pltpu.VMEM((outer, size, quarter), F32),
            pltpu.VMEM((size, quarter), F32),
            pltpu.VMEM((inner, size, quarter), F32),
            pltpu.VMEM((size, quarter), F32),
            pltpu.VMEM((inner, size, quarter), F32),
            pltpu.VMEM((8, LANES), F32),
            pltpu.VMEM((inner, 8, LANES), F32),
            pltpu.VMEM((inner, size, rows), F32),
            pltpu.VMEM((inner, size, rows), F32),
            pltpu.VMEM((outer, trades, feats), BF16),
            pltpu.VMEM((outer, trades, feats), BF16),
            pltpu.VMEM((inner, rows, feats), BF16),
            pltpu.VMEM((inner, rows, feats), BF16),
            pltpu.VMEM((inner * rows, outer * trades), F32),
            pltpu.VMEM((inner * rows, outer * trades), BF16),
            pltpu.VMEM((trades, feats), BF16),
            pltpu.SemaphoreType.DMA((7,)),
            pltpu.SemaphoreType.DMA((5, z_pairs)),
            pltpu.SemaphoreType.DMA((5, z_pairs)),
            pltpu.SemaphoreType.DMA((8, q_pairs)),
            pltpu.SemaphoreType.DMA((8, q_pairs)),
            pltpu.SemaphoreType.DMA((8, PIECES)),
        ],
        compiler_params=pltpu.CompilerParams(
            collective_id=0, has_side_effects=True, vmem_limit_bytes=48 * 1024 * 1024
        ),
    )(
        *(
            pltpu.with_memory_space_constraint(operand, pltpu.HBM)
            for operand in (
                path_basis,
                proxy_weight,
                notional.reshape(1, trades),
                set_of.reshape(-1, trades),
                threshold_index.reshape(inner, quarter),
                threshold_levels,
                loss_rate.reshape(inner, quarter),
            )
        )
    )
    return loss[0, :1], basis_adjoint, weight_adjoint


def solution(mesh):
    placed = (
        P(("groups", "paths"), None),
        P(("groups", "paths"), None),
        P(("groups", "paths")),
        P("groups"),
        P("groups"),
        P("groups"),
        P("groups"),
    )
    return jax.shard_map(
        shards,
        mesh=mesh,
        in_specs=placed,
        out_specs=(P("groups"), P(("groups", "paths"), None), P(("groups", "paths"), None)),
        check_vma=False,
    )
```

```python
import functools
import math

import jax
import jax.numpy as jnp
from jax import lax
from jax.experimental import pallas as pl
from jax.experimental.pallas import tpu as pltpu
from jax.sharding import PartitionSpec as P

REGRESSORS = 32
RIDGE_SCALE = 0.01
PRECISE = lax.Precision.HIGHEST
LANES = 128
PIECES = 4
F32 = jnp.float32
BF16 = jnp.bfloat16

NN = (((1,), (0,)), ((), ()))
NT = (((1,), (1,)), ((), ()))
TN = (((0,), (0,)), ((), ()))


def mm(a, b, dims=NN):
    return lax.dot_general(a, b, dims, preferred_element_type=F32)


def precise(a, b, dims=NN):
    return lax.dot_general(a, b, dims, precision=PRECISE, preferred_element_type=F32)


def split3(x):
    hi = x.astype(BF16)
    rest = x - hi.astype(F32)
    mid = rest.astype(BF16)
    lo = (rest - mid.astype(F32)).astype(BF16)
    return hi, mid, lo


def stack3(x):
    hi, mid, lo = split3(x)
    return jnp.concatenate([hi, mid, lo, jnp.zeros_like(hi)], axis=0)


def design_of(basis):
    front = pltpu.roll(basis[:, :LANES].astype(F32), 1, 1)
    lane = lax.broadcasted_iota(jnp.int32, front.shape, 1)
    return jnp.where(lane == 0, 1.0, jnp.where(lane < REGRESSORS, front, 0.0))


def triple(design):
    return (
        design + pltpu.roll(design, REGRESSORS, 1) + pltpu.roll(design, 2 * REGRESSORS, 1)
    ).astype(BF16)


def spd_inverse(gram, between):
    size = REGRESSORS
    row = lax.broadcasted_iota(jnp.int32, (size, LANES), 0)
    lane = lax.broadcasted_iota(jnp.int32, (size, LANES), 1)
    work = jnp.where(lane < size, gram, jnp.where(lane == row + size, 1.0, 0.0))
    for k in range(size):
        if k == size // 3:
            between()
        column = jnp.broadcast_to(work[:, k : k + 1], work.shape)
        pivot = work[k : k + 1, :] / column[k : k + 1, :]
        work = jnp.where(row == k, pivot, work - column * pivot)
    return pltpu.roll(work, LANES - size, 1)


def set_table(labels, set_total):
    sets = lax.broadcasted_iota(jnp.int32, (set_total, labels.shape[1]), 0)
    return jnp.where(sets == labels, 1.0, 0.0).astype(BF16)


def partner(index, step, count):
    if count & (count - 1):
        return lax.rem(index + step, count)
    result, weight = 0, 1
    while weight < count:
        bit = lax.rem(lax.div(index, weight), 2)
        result = result + weight * (1 - bit if step & weight else bit)
        weight *= 2
    return result


def kernel(
    inner, outer, paths_all, set_total,
    pb_hbm, w_hbm, not_hbm, set_hbm, tidx_hbm, level_hbm, rate_hbm,
    loss_ref, basis_ref, wadj_ref,
    not_ref, set_ref, tidx_ref, level_ref, rate_ref,
    pall, wall, nall, nsend, gown, gall, gq, dstack, table, invert,
    bown, bq, bzsend, bz, csend, cq, ssend, sq, lsend, lq,
    eown, eq, wown, wz, pown, pq, nsig, tval, sval,
    via, local, zsend, zrecv, qsend, qrecv, steps,
):
    rows, feats = basis_ref.shape
    trades = wadj_ref.shape[0]
    quarter = set_total // inner
    me = lax.axis_index("paths")
    q = lax.rem(me, inner)
    z = lax.div(me, inner)

    loads = [
        pltpu.make_async_copy(source, target, local.at[i])
        for i, (source, target) in enumerate(
            [
                (pb_hbm, pall.at[q]),
                (not_hbm, not_ref),
                (w_hbm, wall.at[z]),
                (set_hbm, set_ref),
                (tidx_hbm, tidx_ref),
                (level_hbm, level_ref),
                (rate_hbm, rate_ref),
            ]
        )
    ]
    for load in loads:
        load.start()

    barrier = pltpu.get_barrier_semaphore()
    for d in range(1, inner):
        pl.semaphore_signal(
            barrier, inc=1, device_id={"paths": z * inner + lax.rem(q + d, inner)},
            device_id_type=pl.DeviceIdType.MESH,
        )
    for d in range(1, outer):
        pl.semaphore_signal(
            barrier, inc=1, device_id={"paths": lax.rem(z + d, outer) * inner + q},
            device_id_type=pl.DeviceIdType.MESH,
        )

    pending = []

    def over_q(which, source, target):
        copies = []
        for d in range(inner - 1, 0, -1):
            peer = partner(q, d, inner)
            copy = pltpu.make_async_remote_copy(
                src_ref=source(peer), dst_ref=target.at[q],
                send_sem=qsend.at[which, d - 1], recv_sem=qrecv.at[which, d - 1],
                device_id={"paths": z * inner + peer},
                device_id_type=pl.DeviceIdType.MESH,
            )
            copy.start()
            copies.append(copy)
        pending.extend(copies)
        return copies

    def over_z(which, source, target):
        copies = []
        for d in range(outer - 1, 0, -1):
            peer = partner(z, d, outer)
            copy = pltpu.make_async_remote_copy(
                src_ref=source(peer), dst_ref=target.at[z],
                send_sem=zsend.at[which, d - 1], recv_sem=zrecv.at[which, d - 1],
                device_id={"paths": peer * inner + q},
                device_id_type=pl.DeviceIdType.MESH,
            )
            copy.start()
            copies.append(copy)
        pending.extend(copies)
        return copies

    def arrive(copies):
        for copy in copies:
            copy.wait_recv()

    relay = outer == 4 and trades % LANES == 0
    part = trades // PIECES
    edge = z * (3 - z) == 0
    near, far, mid = partner(z, 1, outer), partner(z, 2, outer), partner(z, 3, outer)

    def piece(source, target, p, row, peer):
        cut = pl.ds(p * part, part)
        return pltpu.make_async_remote_copy(
            src_ref=source.at[cut], dst_ref=target.at[cut],
            send_sem=steps.at[row, p], recv_sem=steps.at[row + 1, p],
            device_id={"paths": peer * inner + q}, device_id_type=pl.DeviceIdType.MESH,
        )

    def block(source, target, which, lane, peer):
        return pltpu.make_async_remote_copy(
            src_ref=source, dst_ref=target,
            send_sem=zsend.at[which, lane], recv_sem=zrecv.at[which, lane],
            device_id={"paths": peer * inner + q}, device_id_type=pl.DeviceIdType.MESH,
        )

    def total(ref, count):
        result = ref[0].astype(F32)
        for i in range(1, count):
            result = result + ref[i].astype(F32)
        return result

    loads[0].wait()
    own_design = design_of(pall[q])
    own_triple = triple(own_design)
    own_turned = jnp.transpose(own_design)[:REGRESSORS, :].astype(BF16)
    gown[...] = own_turned
    loads[1].wait()
    nrow = jnp.broadcast_to(not_ref[...].astype(F32), (8, trades))
    nsend[...] = nrow
    loads[2].wait()
    pl.semaphore_wait(barrier, inner + outer - 2)

    gram_z = over_z(0, lambda peer: gown, gall)
    note_z = over_z(1, lambda peer: nsend, nall)
    if relay:
        far_in = [piece(wall.at[z], wall.at[z], p, 0, far) for p in range(PIECES)]
        near_in = block(wall.at[z], wall.at[z], 2, 0, near)
        mid_in = block(wall.at[z], wall.at[z], 2, 1, mid)
        handed = [piece(wall.at[far], wall.at[far], p, 2, near) for p in range(PIECES)]
        for copy in far_in:
            copy.start()
        near_in.start()
        pending.extend(far_in + [near_in])

        @pl.when(jnp.logical_not(edge))
        def _():
            mid_in.start()
    else:
        trade_z = over_z(2, lambda peer: wall.at[z], wall)

    def forward(p):
        if relay:
            far_in[p].wait_recv()

            @pl.when(jnp.logical_not(edge))
            def _():
                handed[p].start()

    path_q = over_q(0, lambda peer: pall.at[q], pall)
    gall[z] = own_turned
    nall[z] = nrow

    arrive(gram_z)
    gram_q = over_q(1, lambda peer: gall, gq)
    gq[q] = gall[...]

    for load in loads[3:]:
        load.wait()
    all_levels = tidx_ref[...]
    all_thresholds = jnp.zeros((inner, quarter), F32)
    levels = tidx_ref[pl.ds(q, 1), :]
    thresholds = jnp.zeros((1, quarter), F32)
    for i in range(level_ref.shape[0]):
        thresholds = jnp.where(levels == i, level_ref[i], thresholds)
        all_thresholds = jnp.where(all_levels == i, level_ref[i], all_thresholds)
    thresholds = jnp.transpose(jnp.broadcast_to(thresholds, (quarter, quarter)))[:, :1]
    rate = jnp.transpose(
        jnp.broadcast_to(rate_ref[pl.ds(q, 1), :], (quarter, quarter))
    )[:, :1]
    all_rates = rate_ref[...]
    labels = jnp.concatenate(
        [set_ref[pl.ds(i * inner + q, 1), :] for i in range(outer)], axis=1
    )
    table[...] = set_table(labels, set_total)

    forward(0)
    arrive(path_q)
    paths = pall[...].reshape(inner * rows, feats)
    design = design_of(paths)
    design3 = triple(design)
    design_t = jnp.transpose(design)[:REGRESSORS, :].astype(BF16)

    forward(1)
    arrive(gram_q)
    turned_all = jnp.concatenate(
        [gq[i, j] for i in range(inner) for j in range(outer)], axis=1
    )
    dstack[...] = jnp.concatenate(
        [turned_all, turned_all, turned_all, jnp.zeros_like(turned_all)], axis=0
    )
    gram = mm(turned_all, dstack[...], NT)
    forward(2)
    gram_row = lax.broadcasted_iota(jnp.int32, (REGRESSORS, LANES), 0)
    gram_lane = lax.broadcasted_iota(jnp.int32, (REGRESSORS, LANES), 1)
    ridge = jnp.where(gram_row == gram_lane, RIDGE_SCALE * paths_all, 0.0)
    invert[...] = spd_inverse(gram + ridge, lambda: forward(3))

    arrive(note_z)
    notional = jnp.concatenate([nall[i][0:1, :] for i in range(outer)], axis=1)
    if relay:
        near_in.wait_recv()

        @pl.when(jnp.logical_not(edge))
        def _():
            mid_in.wait_recv()

        @pl.when(edge)
        def _():
            for copy in handed:
                copy.wait_recv()
    else:
        arrive(trade_z)
    weights = wall[...].reshape(outer * trades, feats)
    pre_act = mm(paths, weights, NT)
    small = jnp.exp(-jnp.abs(pre_act))
    tval[...] = (notional * (jnp.maximum(pre_act, 0.0) + jnp.log1p(small))).astype(BF16)

    by_trade = mm(design_t, tval[...])
    by_set = mm(jnp.concatenate(split3(by_trade), axis=0), table[...], NT)
    moments = (
        by_set[:REGRESSORS] + by_set[REGRESSORS : 2 * REGRESSORS] + by_set[2 * REGRESSORS :]
    )
    for i in range(inner):
        bown[i] = moments[:, i * quarter : (i + 1) * quarter]
    moment_q = over_q(2, lambda peer: bown.at[peer], bq)
    bq[q] = bown[q]
    nsig[...] = notional * (jnp.where(pre_act >= 0.0, 1.0, small) / (1.0 + small))
    arrive(moment_q)
    moment_mid = total(bq, inner)
    bzsend[...] = moment_mid
    moment_z = over_z(3, lambda peer: bzsend, bz)
    bz[z] = moment_mid
    arrive(moment_z)
    inverse = invert[:, :REGRESSORS]
    coeffs = precise(inverse, total(bz, outer))
    csend[...] = coeffs
    coeffs_q = over_q(3, lambda peer: csend, cq)
    cq[q] = coeffs
    excess = mm(stack3(coeffs), dstack[...], TN) - thresholds
    fade = jnp.exp(-jnp.abs(excess))
    seed = rate * (jnp.where(excess >= 0.0, 1.0, fade) / (1.0 + fade))
    seed_cut = mm(dstack[:REGRESSORS, :], jnp.concatenate(split3(seed), axis=0), NT)
    seed_sum = (
        seed_cut[:, :quarter] + seed_cut[:, quarter : 2 * quarter] + seed_cut[:, 2 * quarter :]
    )
    solved = precise(inverse, seed_sum)
    ssend[...] = solved
    answer_q = over_q(4, lambda peer: ssend, sq)
    sq[q] = solved
    loss = jnp.maximum(excess, 0.0) + jnp.log1p(fade)
    loss_part = jnp.sum(rate * jnp.sum(loss, axis=1, keepdims=True), axis=0, keepdims=True)
    loss_row = jnp.broadcast_to(loss_part, (8, LANES))
    lsend[...] = loss_row
    loss_q = over_q(7, lambda peer: lsend, lq)
    lq[q] = loss_row
    arrive(coeffs_q)
    coeffs_all = jnp.concatenate([cq[i] for i in range(inner)], axis=1)
    arrive(answer_q)
    solved_all = jnp.concatenate([sq[i] for i in range(inner)], axis=1)

    picked = mm(jnp.concatenate(split3(solved_all), axis=0), table[...])
    solved3 = jnp.concatenate(
        [picked.astype(BF16), jnp.zeros((LANES - 3 * REGRESSORS, picked.shape[1]), BF16)], axis=0
    )
    spread = mm(design3, solved3).astype(BF16).astype(F32)
    slopes = (nsig[...] * spread).astype(BF16)
    scale = 1.0 / math.sqrt(paths_all)
    sval[...] = slopes

    def weigh(i):
        columns = pl.ds(pl.multiple_of(i * trades, LANES), trades)
        wown[i] = (mm(sval[:, columns], paths, TN) * scale).astype(BF16)

    if not relay:
        weight_part = mm(slopes, paths, TN) * scale
        wown[...] = weight_part.astype(BF16).reshape(outer, trades, feats)
    if relay:
        carried = [piece(wown.at[mid], via, p, 6, near) for p in range(PIECES)]
        far_out = [piece(wown.at[far], wz.at[z], p, 4, far) for p in range(PIECES)]
        near_out = block(wown.at[near], wz.at[z], 4, 0, near)
        mid_out = block(wown.at[mid], wz.at[z], 4, 1, mid)

        weigh(mid)

        @pl.when(edge)
        def _():
            for copy in carried:
                copy.start()
            wz[mid] = jnp.zeros_like(via)

        @pl.when(jnp.logical_not(edge))
        def _():
            mid_out.start()

        weigh(far)

        @pl.when(edge)
        def _():
            for copy in far_out:
                copy.start()

        weigh(near)
        near_out.start()
        weigh(z)
        pending.extend(far_out + [near_out])
    else:
        weight_z = over_z(4, lambda peer: wown.at[peer], wz)
    wz[z] = wown[z]

    pulled = mm(solved3, tval[...], NT)
    pulled = (
        pulled[:REGRESSORS]
        + pulled[REGRESSORS : 2 * REGRESSORS]
        + pulled[2 * REGRESSORS : 3 * REGRESSORS]
    )
    for i in range(inner):
        eown[i] = pulled[:, i * rows : (i + 1) * rows]
    pull_q = over_q(5, lambda peer: eown.at[peer], eq)
    eq[q] = eown[q]
    basis_part = mm(slopes, weights)
    pown[...] = basis_part.astype(BF16).reshape(inner, rows, feats)
    basis_q = over_q(6, lambda peer: pown.at[peer], pq)
    pq[q] = pown[q]

    if relay:

        @pl.when(jnp.logical_not(edge))
        def _():
            for p in range(PIECES):
                carried[p].wait_recv()
                cut = pl.ds(p * part, part)
                joint = wown[far, cut, :].astype(F32) + via[cut, :].astype(F32)
                wown[far, cut, :] = joint.astype(BF16)
                far_out[p].start()

    fitted = mm(own_triple, stack3(coeffs_all))
    full_thresholds = jnp.concatenate([all_thresholds[i : i + 1] for i in range(inner)], axis=1)
    full_rates = jnp.concatenate([all_rates[i : i + 1] for i in range(inner)], axis=1)
    over = fitted - full_thresholds
    tail = jnp.exp(-jnp.abs(over))
    own_seed = full_rates * (jnp.where(over >= 0.0, 1.0, tail) / (1.0 + tail))
    residual = own_seed - mm(own_triple, stack3(solved_all))
    term = precise(coeffs_all, residual, NT) - precise(solved_all, fitted, NT)
    arrive(loss_q)
    loss_ref[...] = total(lq, inner)[:1] / (paths_all * set_total)
    arrive(pull_q)
    term = term + total(eq, inner)
    padded = jnp.concatenate([term, jnp.zeros((LANES - REGRESSORS, rows), F32)], axis=0)
    turned = pltpu.roll(jnp.transpose(padded), LANES - 1, 1)
    lane = lax.broadcasted_iota(jnp.int32, turned.shape, 1)
    turned = jnp.where(lane < REGRESSORS - 1, turned, 0.0)
    arrive(basis_q)
    basis_ref[...] = total(pq, inner)
    basis_ref[:, :LANES] = basis_ref[:, :LANES] + turned
    if relay:
        arrive(far_out)
        near_out.wait_recv()

        @pl.when(jnp.logical_not(edge))
        def _():
            mid_out.wait_recv()
            mid_out.wait_send()
            mid_in.wait_send()
            for copy in handed:
                copy.wait_send()

        @pl.when(edge)
        def _():
            for copy in carried:
                copy.wait_send()
    else:
        arrive(weight_z)
    wadj_ref[...] = total(wz, outer)
    for copy in pending:
        copy.wait_send()


def shards(
    path_basis, proxy_weight, notional, set_of, threshold_index, threshold_levels, loss_rate
):
    count = lax.axis_size("paths")
    inner = math.gcd(4, count)
    outer = count // inner
    rows, feats = path_basis.shape
    trades = proxy_weight.shape[0]
    set_total = loss_rate.shape[0]
    quarter = set_total // inner
    size = REGRESSORS
    vmem = pl.BlockSpec(memory_space=pltpu.VMEM)
    z_pairs, q_pairs = max(outer - 1, 1), max(inner - 1, 1)
    loss, basis_adjoint, weight_adjoint = pl.pallas_call(
        functools.partial(kernel, inner, outer, rows * count, set_total),
        out_shape=(
            jax.ShapeDtypeStruct((1, LANES), F32),
            jax.ShapeDtypeStruct((rows, feats), F32),
            jax.ShapeDtypeStruct((trades, feats), F32),
        ),
        in_specs=[pl.BlockSpec(memory_space=pltpu.HBM)] * 7,
        out_specs=(vmem, vmem, vmem),
        scratch_shapes=[
            pltpu.VMEM((1, trades), BF16),
            pltpu.VMEM((inner * outer, trades), jnp.int32),
            pltpu.VMEM((inner, quarter), jnp.int32),
            pltpu.SMEM(threshold_levels.shape, F32),
            pltpu.VMEM((inner, quarter), F32),
            pltpu.VMEM((inner, rows, feats), BF16),
            pltpu.VMEM((outer, trades, feats), BF16),
            pltpu.VMEM((outer, 8, trades), F32),
            pltpu.VMEM((8, trades), F32),
            pltpu.VMEM((size, rows), BF16),
            pltpu.VMEM((outer, size, rows), BF16),
            pltpu.VMEM((inner, outer, size, rows), BF16),
            pltpu.VMEM((LANES, count * rows), BF16),
            pltpu.VMEM((set_total, outer * trades), BF16),
            pltpu.VMEM((size, LANES), F32),
            pltpu.VMEM((inner, size, quarter), F32),
            pltpu.VMEM((inner, size, quarter), F32),
            pltpu.VMEM((size, quarter), F32),
            pltpu.VMEM((outer, size, quarter), F32),
            pltpu.VMEM((size, quarter), F32),
            pltpu.VMEM((inner, size, quarter), F32),
            pltpu.VMEM((size, quarter), F32),
            pltpu.VMEM((inner, size, quarter), F32),
            pltpu.VMEM((8, LANES), F32),
            pltpu.VMEM((inner, 8, LANES), F32),
            pltpu.VMEM((inner, size, rows), F32),
            pltpu.VMEM((inner, size, rows), F32),
            pltpu.VMEM((outer, trades, feats), BF16),
            pltpu.VMEM((outer, trades, feats), BF16),
            pltpu.VMEM((inner, rows, feats), BF16),
            pltpu.VMEM((inner, rows, feats), BF16),
            pltpu.VMEM((inner * rows, outer * trades), F32),
            pltpu.VMEM((inner * rows, outer * trades), BF16),
            pltpu.VMEM((inner * rows, outer * trades), BF16),
            pltpu.VMEM((trades, feats), BF16),
            pltpu.SemaphoreType.DMA((7,)),
            pltpu.SemaphoreType.DMA((5, z_pairs)),
            pltpu.SemaphoreType.DMA((5, z_pairs)),
            pltpu.SemaphoreType.DMA((8, q_pairs)),
            pltpu.SemaphoreType.DMA((8, q_pairs)),
            pltpu.SemaphoreType.DMA((8, PIECES)),
        ],
        compiler_params=pltpu.CompilerParams(
            collective_id=0, has_side_effects=True, vmem_limit_bytes=48 * 1024 * 1024
        ),
    )(
        *(
            pltpu.with_memory_space_constraint(operand, pltpu.HBM)
            for operand in (
                path_basis,
                proxy_weight,
                notional.reshape(1, trades),
                set_of.reshape(-1, trades),
                threshold_index.reshape(inner, quarter),
                threshold_levels,
                loss_rate.reshape(inner, quarter),
            )
        )
    )
    return loss[0, :1], basis_adjoint, weight_adjoint


def solution(mesh):
    placed = (
        P(("groups", "paths"), None),
        P(("groups", "paths"), None),
        P(("groups", "paths")),
        P("groups"),
        P("groups"),
        P("groups"),
        P("groups"),
    )
    return jax.shard_map(
        shards,
        mesh=mesh,
        in_specs=placed,
        out_specs=(P("groups"), P(("groups", "paths"), None), P(("groups", "paths"), None)),
        check_vma=False,
    )
```
